32 devices in a mesh: gx: 4 (over y, x), gy: 8 (over z, core).
Axes of the slice: x: 2, y: 2, z: 4, core: 2. Of those that a mesh axis runs over, the one named last changes fastest.
Arguments:
- levels: int32 [8, 64, 8192], P(None, 'gx', 'gy'), may hold values from 0 to 7
- probe_bits: int32 [8, 8, 64, 8192], P(None, None, 'gx', 'gy'), may hold values from 0 to 1
Outputs:
- green: float32 [2, 8192, 64], P(None, ('gx', 'gy'))
- last_vector: float32 [8, 8, 64, 8192], P(None, None, 'gx', 'gy')
The draws below stay inside these ranges and needn't reach their ends.
All inputs are finite; a program needn't handle non-finite values.
Results may differ from the reference program's by a relative error of at most 0.00011.
Values sent between devices are 32-bit elements; how exact they have to be, the bound alone decides.
No kernel may reach another device: no remote copies, remote signals or barrier semaphores. Data moves between devices by JAX's collectives and lax.ppermute only.
A program may use at most 128 MiB of HBM per device.

```python
import math
import jax
import jax.numpy as jnp
from jax import lax

PROBES = 8
PL = 8
STEPS = 4
LEVELS = 8
NE = 8192
NMOM = 8
NX = 64
NY = 8192
SITES = 4194304


def draw_levels(key, part):
    plane_key, span_key, fine_key = jax.random.split(jax.random.fold_in(key, 11), 3)
    base = jax.random.randint(plane_key, (PL, 1, 1), 0, LEVELS)
    span = jax.random.randint(span_key, (PL, 1, 1), 2, LEVELS + 1)
    fine = jax.random.randint(fine_key, (PL, NX, NY), 0, 1 << 20)
    return ((base + fine % span) % LEVELS).astype(jnp.int32)


def draw_probe_bits(key, part):
    coarse_key, rate_key, flip_key = jax.random.split(jax.random.fold_in(key, 23), 3)
    coarse = jax.random.randint(coarse_key, (PL, NX // 2, NY // 4), 0, 2)
    common = jnp.repeat(jnp.repeat(coarse, 2, axis=1), 4, axis=2)
    rates = jax.random.randint(rate_key, (PROBES, 1, 1, 1), 1, 8)
    flips = (jax.random.randint(flip_key, (PROBES, PL, NX, NY), 0, 16) < rates).astype(jnp.int32)
    return ((common[None] + flips) % 2).astype(jnp.int32)


def block_levels(rng, shape, cuts, least, high):
    level, own = 1.0, jax.random.fold_in(rng, 6)
    for dim, parts in cuts:
        draws = jnp.exp(jax.random.uniform(jax.random.fold_in(own, dim), (parts,), jnp.float32, least / len(cuts), high / len(cuts)))
        level = level * jnp.repeat(draws, shape[dim] // parts).reshape([-1 if axis == dim else 1 for axis in range(len(shape))])
    return level


def setup_inputs(seed: int = 0) -> dict:
    streams_of = jax.random.split(jax.random.key(seed), 3)
    return {
        "levels": draw_levels(jax.random.fold_in(streams_of[2], 71), 0),
        "probe_bits": draw_probe_bits(jax.random.fold_in(streams_of[2], 71), 0),
    }


disorder_width = 4.0
field_strength = 3.0
spectral_scale = 10.0
energy_edge = 0.9


def jackson_weights(count):
    total = count + 1.0
    values = []
    for order in range(count):
        damping = ((count - order + 1.0) * math.cos(math.pi * order / total) + math.sin(math.pi * order / total) / math.tan(math.pi / total)) / total
        values.append(damping if order == 0 else 2.0 * damping)
    return jnp.asarray(values, dtype=jnp.float32)


def energy_tables(energy_index, count, total_energies):
    phase = math.pi * (energy_index.astype(jnp.float32) + 0.5) / total_energies
    theta = jnp.arccos(energy_edge * jnp.cos(phase))
    orders = jnp.arange(count).astype(jnp.float32)
    weights = jackson_weights(count)
    angles = theta[:, None] * orders[None, :]
    denominator = jnp.sin(theta)[:, None]
    real_part = -weights[None, :] * jnp.sin(angles) / denominator
    imag_part = -weights[None, :] * jnp.cos(angles) / denominator
    return real_part, imag_part


def hopping(field, onsite):
    beside = jnp.roll(field, -1, 2) + jnp.roll(field, 1, 2)
    beside = beside + jnp.roll(field, -1, 3) + jnp.roll(field, 1, 3)
    zeros_plane = jnp.zeros_like(field[:, :1])
    beside = beside + jnp.concatenate([field[:, 1:], zeros_plane], 1)
    beside = beside + jnp.concatenate([zeros_plane, field[:, :-1]], 1)
    return (onsite[None] * field - beside) / spectral_scale


def inner_matrix(first, second):
    left = first.reshape(first.shape[0], -1)
    right = second.reshape(second.shape[0], -1)
    return jnp.dot(left, right.T, precision=lax.Precision.HIGHEST, preferred_element_type=jnp.float32)


def moments_from(grams, sites):
    first = grams[0] / sites
    second = grams[1] / sites
    result = [first, second]
    for order in range(1, grams.shape[0] // 2):
        result.append(2.0 * grams[2 * order] / sites - first)
        result.append(2.0 * grams[2 * order + 1] / sites - second)
    stacked = jnp.stack(result)
    return stacked.reshape(stacked.shape[0], -1)


def reference(levels, probe_bits):
    row_index = jnp.arange(NX).astype(jnp.float32)
    onsite = disorder_width * (levels.astype(jnp.float32) / (LEVELS - 1) - 0.5) + field_strength * ((row_index + 0.5) / NX - 0.5)[None, :, None]
    vectors = [(2 * probe_bits - 1).astype(jnp.float32)]
    for step in range(STEPS):
        hopped = hopping(vectors[-1], onsite)
        if step == 0:
            vectors.append(hopped)
        else:
            vectors.append(2.0 * hopped - vectors[-2])
    grams = []
    for step in range(STEPS):
        grams.append(inner_matrix(vectors[step], vectors[step]))
        grams.append(inner_matrix(vectors[step], vectors[step + 1]))
    moments = moments_from(jnp.stack(grams), SITES)
    real_part, imag_part = energy_tables(jnp.arange(NE).astype(jnp.int32), NMOM, NE)
    green_real = jnp.dot(real_part, moments, precision=lax.Precision.HIGHEST, preferred_element_type=jnp.float32)
    green_imag = jnp.dot(imag_part, moments, precision=lax.Precision.HIGHEST, preferred_element_type=jnp.float32)
    return jnp.stack([green_real, green_imag]), vectors[-1]
```

```python
import functools
import math

import jax
import jax.numpy as jnp
from jax import lax
from jax.experimental import pallas as pl
from jax.experimental.pallas import tpu as pltpu
from jax.sharding import PartitionSpec as P

STEPS = 4
LEVELS = 8
NE = 8192
NMOM = 2 * STEPS
LANES = 128
SUB = 8

disorder_width = 4.0
field_strength = 3.0
spectral_scale = 10.0
energy_edge = 0.9

F32 = jnp.float32


def tile_view(array):
    rows, cols = array.shape[-2:]
    split = array.reshape(-1, rows // SUB, SUB, cols // LANES, LANES)
    return split.transpose(0, 1, 3, 2, 4).reshape(-1, LANES)


def untile_view(view, shape):
    rows, cols = shape[-2:]
    split = view.reshape(-1, rows // SUB, cols // LANES, SUB, LANES)
    return split.transpose(0, 1, 3, 2, 4).reshape(shape)


class Dims:
    def __init__(self, levels, bits, gx):
        self.q = bits.shape[0]
        self.pl, self.rows, self.cols = levels.shape
        self.ct = self.cols // LANES
        self.width = self.cols + LANES
        self.total_rows = self.rows * gx
        self.plane_rows = self.rows * self.ct
        self.probe_rows = self.pl * self.plane_rows

    def tile_row(self, row, col_tile):
        return (row // SUB) * (self.ct * SUB) + col_tile * SUB + row % SUB

    def load_v0(self, bits_ref, row, plane, col_tile):
        start = plane * self.plane_rows + self.tile_row(row, col_tile)
        bits = bits_ref[pl.ds(start, self.q, stride=self.probe_rows), :]
        return (2 * bits - 1).astype(F32)

    def load_onsite(self, levels_ref, first_row, row, col_tile):
        start = self.tile_row(row, col_tile)
        level = levels_ref[pl.ds(start, self.pl, stride=self.plane_rows), :]
        index = (first_row + row).astype(F32)
        field = field_strength * ((index + 0.5) / self.total_rows - 0.5)
        onsite = disorder_width * (level.astype(F32) / (LEVELS - 1) - 0.5) + field
        return onsite * (2.0 / spectral_scale)


def prepare_kernel(d, first_ref, bits_ref, levels_ref, up_ref, down_ref, right_ref, left_ref):
    first_row = first_ref[0]
    for k in range(STEPS):
        for ref, row in ((up_ref, d.rows - STEPS + k), (down_ref, k)):
            for t in range(d.ct):
                lanes = slice(t * LANES, (t + 1) * LANES)
                for p in range(d.pl):
                    ref[k * d.pl + p, :, lanes] = d.load_v0(bits_ref, row, p, t)
    for k in range(STEPS - 1):
        for ref, row in ((up_ref, d.rows - STEPS + 1 + k), (down_ref, k)):
            for t in range(d.ct):
                lanes = slice(t * LANES, (t + 1) * LANES)
                ref[STEPS * d.pl + k, :, lanes] = d.load_onsite(levels_ref, first_row, row, t)
    for row in range(d.rows):
        for ref, t in ((right_ref, d.ct - 1), (left_ref, 0)):
            for p in range(d.pl):
                ref[row * d.pl + p] = d.load_v0(bits_ref, row, p, t)
            ref[d.rows * d.pl + row] = d.load_onsite(levels_ref, first_row, row, t)


def edge_mask(shape):
    lane = lax.broadcasted_iota(jnp.int32, shape, len(shape) - 1)
    return lane < STEPS, lane >= LANES - STEPS


def merge_kernel(d, before_ref, after_ref, side_ref, up_ref, down_ref):
    count = d.rows * d.pl

    def merged(i):
        low, high = edge_mask((SUB, LANES))
        return jnp.where(low, after_ref[i], jnp.where(high, before_ref[i], 0.0))

    for i in range(count + d.rows):
        side_ref[i] = merged(i)
    for ref, v_first, o_first in (
        (up_ref, d.rows - STEPS, d.rows - STEPS + 1),
        (down_ref, 0, 0),
    ):
        items = [merged((v_first + k) * d.pl + p) for k in range(STEPS) for p in range(d.pl)]
        items += [merged(count + o_first + k) for k in range(STEPS - 1)]
        per = LANES // (2 * STEPS)
        for base in range(0, len(items), per):
            total = None
            for g, item in enumerate(items[base : base + per]):
                moved = pltpu.roll(item, (STEPS + 2 * STEPS * g) % LANES, 1)
                total = moved if total is None else total + moved
            ref[base // per] = total


def unpack_side(ref, index):
    per = LANES // (2 * STEPS)
    g = index % per
    low, high = edge_mask((SUB, LANES))
    moved = pltpu.roll(ref[index // per], (-(STEPS + 2 * STEPS * g)) % LANES, 1)
    return jnp.where(low | high, moved, 0.0)


def row_step(d, n, center, above, below, prev, onsite, out):
    hop = 2.0 / spectral_scale
    for p in range(d.pl):
        x = center(p)
        beside = above(p) + below(p)
        beside = beside + pltpu.roll(x, 1, 1) + pltpu.roll(x, d.width - 1, 1)
        if p + 1 < d.pl:
            beside = beside + center(p + 1)
        if p > 0:
            beside = beside + center(p - 1)
        value = onsite(p) * x - hop * beside
        out(p, 0.5 * value if n == 1 else value - prev(p))


def split_pair(x):
    high = x.astype(jnp.bfloat16).astype(F32)
    return high, x - high


def gram_row(d, vectors):
    total = None
    for p in range(d.pl):
        v = [get(p)[:, : d.cols] for get in vectors]
        halves = [split_pair(x) for x in v[1:]]
        right = [v[0], v[0]]
        for pair in halves:
            right += list(pair)
        left = [v[0], halves[STEPS - 2][0], halves[STEPS - 2][1], halves[STEPS - 2][1]]
        right = jnp.concatenate(right, 0).astype(jnp.bfloat16)
        left = jnp.concatenate(left, 0).astype(jnp.bfloat16)
        part = lax.dot_general(
            left, right, (((1,), (1,)), ((), ())), preferred_element_type=F32
        )
        total = part if total is None else total + part
    return total


def store_output(d, out_ref, row, plane, value):
    for t in range(d.ct):
        start = plane * d.plane_rows + d.tile_row(row, t)
        out_ref[pl.ds(start, d.q, stride=d.probe_rows), :] = value[:, t * LANES : (t + 1) * LANES]


def interior_kernel(d, first_ref, bits_ref, levels_ref, side_ref, *refs):
    v = refs[:STEPS]
    ons, out_ref, gram_ref = refs[STEPS:]
    first_row = first_ref[0]

    def fill(row, _):
        for p in range(d.pl):
            for t in range(d.ct):
                v[0][row + STEPS, p, :, t * LANES : (t + 1) * LANES] = d.load_v0(bits_ref, row, p, t)
            v[0][row + STEPS, p, :, d.cols :] = side_ref[row * d.pl + p]
        for t in range(d.ct):
            ons[row + STEPS, :, t * LANES : (t + 1) * LANES] = d.load_onsite(
                levels_ref, first_row, row, t
            )
        ons[row + STEPS, :, d.cols :] = side_ref[d.rows * d.pl + row]
        return 0

    lax.fori_loop(0, d.rows, fill, 0)
    gram_ref[...] = jnp.zeros(gram_ref.shape, F32)
    for n in range(1, STEPS + 1):

        def step(row, _, n=n):
            one_row(d, n, row, v, ons, out_ref, gram_ref)
            return 0

        lax.fori_loop(n, d.rows - n, step, 0)


def one_row(d, n, row, v, ons, out_ref, gram_ref):
    last = []
    at = row + STEPS

    def take(ref, where):
        return lambda p: ref[where, p]

    def out(p, value):
        if n < STEPS:
            v[n][at, p] = value
        else:
            last.append(value)
            store_output(d, out_ref, row, p, value)

    row_step(
        d, n, take(v[n - 1], at), take(v[n - 1], at - 1), take(v[n - 1], at + 1),
        take(v[n - 2], at) if n > 1 else None,
        lambda p: ons[at, pl.ds(p, SUB, stride=0), :], out,
    )
    if n == STEPS:
        gram_ref[...] += gram_row(d, [take(v[m], at) for m in range(STEPS)] + [lambda p: last[p]])


def boundary_kernel(d, before_ref, after_ref, cbefore_ref, cafter_ref, *refs):
    refs = refs[STEPS + 2 :]
    gram_in = refs[0]
    v = refs[1 : 1 + STEPS]
    ons, out_ref, gram_ref, sem = refs[1 + STEPS :]
    copies = []
    sides = ((before_ref, cbefore_ref, 0, 1), (after_ref, cafter_ref, d.rows + STEPS, d.rows + STEPS))
    for index, (rows_ref, _, v_at, o_at) in enumerate(sides):
        for k in range(STEPS):
            copies.append(pltpu.make_async_copy(
                rows_ref.at[pl.ds(k * d.pl, d.pl)], v[0].at[v_at + k, :, :, pl.ds(0, d.cols)],
                sem.at[index, k],
            ))
        for k in range(STEPS - 1):
            copies.append(pltpu.make_async_copy(
                rows_ref.at[STEPS * d.pl + k], ons.at[o_at + k, :, pl.ds(0, d.cols)],
                sem.at[index, STEPS + k],
            ))
    for copy in copies:
        copy.start()
    for _, corner_ref, v_at, o_at in sides:
        for k in range(STEPS):
            for p in range(d.pl):
                v[0][v_at + k, p, :, d.cols :] = unpack_side(corner_ref, k * d.pl + p)
        for k in range(STEPS - 1):
            ons[o_at + k, :, d.cols :] = unpack_side(corner_ref, STEPS * d.pl + k)
    for copy in copies:
        copy.wait()
    gram_ref[...] = gram_in[...]
    for k in range(1, STEPS + 1):
        for n in range(1, STEPS + 1):
            for side in range(2):
                row = n - k if side == 0 else d.rows - 1 - (n - k)
                one_row(d, n, row, v, ons, out_ref, gram_ref)


def flush_kernel(from_ref, to_ref, sem):
    copy = pltpu.make_async_copy(from_ref, to_ref, sem)
    copy.start()
    copy.wait()


def gram_shape(d):
    return (4 * d.q, 2 * (STEPS + 1) * d.q)


def jackson_weights(count):
    total = count + 1.0
    values = []
    for order in range(count):
        damping = (
            (count - order + 1.0) * math.cos(math.pi * order / total)
            + math.sin(math.pi * order / total) / math.tan(math.pi / total)
        ) / total
        values.append(damping if order == 0 else 2.0 * damping)
    return jnp.asarray(values, dtype=F32)


def energy_tables(energy_index, count, total_energies):
    phase = math.pi * (energy_index.astype(F32) + 0.5) / total_energies
    theta = jnp.arccos(energy_edge * jnp.cos(phase))
    orders = jnp.arange(count).astype(F32)
    weights = jackson_weights(count)
    angles = theta[:, None] * orders[None, :]
    denominator = jnp.sin(theta)[:, None]
    real_part = -weights[None, :] * jnp.sin(angles) / denominator
    imag_part = -weights[None, :] * jnp.cos(angles) / denominator
    return jnp.concatenate([real_part, imag_part], 0)


def moments_from(d, gram, sites):
    q = d.q
    zero = gram[:q]
    top, rest = gram[q : 2 * q], gram[2 * q : 3 * q]

    def pair(rows, m):
        return rows[:, 2 * m * q : (2 * m + 1) * q] + rows[:, (2 * m + 1) * q : (2 * m + 2) * q]

    def with_last(m):
        return pair(top, m) + rest[:, 2 * m * q : (2 * m + 1) * q]

    result = [zero[:, :q]] + [pair(zero, m) for m in range(1, STEPS + 1)]
    result.append(2.0 * with_last(STEPS - 2).T - result[1])
    result.append(2.0 * with_last(STEPS - 1) - result[0])
    result.append(2.0 * with_last(STEPS) - result[1])
    return (jnp.stack(result) / sites).reshape(NMOM, q * q)


def add_over(value, axis):
    peers = lax.axis_size(axis)
    if peers & (peers - 1):
        return lax.psum(value, axis)
    shift = 1
    while shift < peers:
        value = value + lax.ppermute(value, axis, [(i, i ^ shift) for i in range(peers)])
        shift *= 2
    return value


VMEM = pl.BlockSpec(memory_space=pltpu.VMEM)
SMEM = pl.BlockSpec(memory_space=pltpu.SMEM)
HBM = pl.BlockSpec(memory_space=pl.ANY)


def params(mib):
    return pltpu.CompilerParams(vmem_limit_bytes=mib * 2**20)


def shift_by(array, axis, step):
    peers = lax.axis_size(axis)
    return lax.ppermute(array, axis, [(i, (i + step) % peers) for i in range(peers)])


def on_device(levels, probe_bits):
    count_gx = lax.axis_size("gx")
    count_gy = lax.axis_size("gy")
    d = Dims(levels, probe_bits, count_gx)
    sites = d.pl * d.total_rows * d.cols * count_gy
    first_row = (lax.axis_index("gx") * d.rows).astype(jnp.int32).reshape(1)
    bits_view = tile_view(probe_bits)
    levels_view = tile_view(levels)
    shape = lambda *dims: jax.ShapeDtypeStruct(dims, F32)
    row_items = STEPS * d.pl + STEPS - 1
    side_items = d.rows * d.pl + d.rows
    corner_tiles = -(-row_items // (LANES // (2 * STEPS)))

    up, down, right, left = pl.pallas_call(
        functools.partial(prepare_kernel, d),
        out_shape=[shape(row_items, SUB, d.cols)] * 2 + [shape(side_items, SUB, LANES)] * 2,
        in_specs=[SMEM, VMEM, VMEM], out_specs=[VMEM] * 4,
        compiler_params=params(24), name="prepare",
    )(first_row, bits_view, levels_view)
    from_left = shift_by(right, "gy", 1)
    from_right = shift_by(left, "gy", -1)
    before = shift_by(up, "gx", 1)
    after = shift_by(down, "gx", -1)
    side, corner_up, corner_down = pl.pallas_call(
        functools.partial(merge_kernel, d),
        out_shape=[shape(side_items, SUB, LANES)] + [shape(corner_tiles, SUB, LANES)] * 2,
        in_specs=[VMEM] * 2, out_specs=[VMEM] * 3,
        compiler_params=params(8), name="merge",
    )(from_left, from_right)
    cbefore = shift_by(corner_up, "gx", 1)
    cafter = shift_by(corner_down, "gx", -1)

    padded = d.rows + 2 * STEPS
    state = [pltpu.VMEM((padded, d.pl, SUB, d.width), F32)] * STEPS
    state += [pltpu.VMEM((padded, d.pl, d.width), F32), pltpu.VMEM(bits_view.shape, F32)]
    *kept, gram = pl.pallas_call(
        functools.partial(interior_kernel, d),
        out_shape=state + [shape(*gram_shape(d))],
        in_specs=[SMEM, VMEM, VMEM, VMEM], out_specs=[VMEM] * (STEPS + 3),
        compiler_params=params(16), name="interior",
    )(first_row, bits_view, levels_view, side)
    *kept, gram = pl.pallas_call(
        functools.partial(boundary_kernel, d),
        out_shape=state + [shape(*gram_shape(d))],
        in_specs=[HBM] * 2 + [VMEM] * (STEPS + 5), out_specs=[VMEM] * (STEPS + 3),
        scratch_shapes=[pltpu.SemaphoreType.DMA((2, 2 * STEPS))],
        input_output_aliases={4 + i: i for i in range(STEPS + 2)},
        compiler_params=params(16), name="boundary",
    )(before, after, cbefore, cafter, *kept, gram)
    last_vector = pl.pallas_call(
        flush_kernel, out_shape=jax.ShapeDtypeStruct(bits_view.shape, F32),
        in_specs=[VMEM], out_specs=HBM, scratch_shapes=[pltpu.SemaphoreType.DMA],
        compiler_params=params(4), name="flush",
    )(kept[-1])
    last_vector = untile_view(last_vector, probe_bits.shape)

    gram = add_over(add_over(gram, "gy"), "gx")
    moments = moments_from(d, gram, sites)
    per_device = NE // (count_gx * count_gy)
    start = (lax.axis_index("gx") * count_gy + lax.axis_index("gy")) * per_device
    tables = energy_tables(start + jnp.arange(per_device), NMOM, NE)
    green = jnp.dot(tables, moments, precision=lax.Precision.HIGHEST, preferred_element_type=F32)
    return green.reshape(2, per_device, d.q * d.q), last_vector


def solution(mesh):
    placed = (P(None, "gx", "gy"), P(None, None, "gx", "gy"))
    return jax.shard_map(
        on_device,
        mesh=mesh,
        in_specs=placed,
        out_specs=(P(None, ("gx", "gy"), None), P(None, None, "gx", "gy")),
        check_vma=False,
    )
```

```python
import functools
import math

import jax
import jax.numpy as jnp
from jax import lax
from jax.experimental import pallas as pl
from jax.experimental.pallas import tpu as pltpu
from jax.sharding import PartitionSpec as P


STEPS = 4
LEVELS = 8
NE = 8192
NMOM = 2 * STEPS
LANES = 128
SUB = 8

disorder_width = 4.0
field_strength = 3.0
spectral_scale = 10.0
energy_edge = 0.9

F32 = jnp.float32


HOP = 2.0 / spectral_scale


def tile_view(array, lead):
    _, cols = array.shape[-2:]
    split = array.reshape(lead + (-1, SUB, cols // LANES, LANES))
    n = len(lead)
    return split.transpose(*range(n + 1), n + 2, n + 1, n + 3).reshape(lead + (-1, LANES))


def untile_view(view, shape):
    rows, cols = shape[-2:]
    split = view.reshape(-1, rows // SUB, cols // LANES, SUB, LANES)
    return split.transpose(0, 1, 3, 2, 4).reshape(shape)


class Rows:
    def __init__(self, ref, offset):
        self.ref, self.offset = ref, offset

    def __getitem__(self, index):
        if isinstance(index, tuple):
            return self.ref[(index[0] + self.offset,) + index[1:]]
        return self.ref[index + self.offset]

    def __setitem__(self, index, value):
        self.ref[(index[0] + self.offset,) + index[1:]] = value

    def rows(self, start, count):
        return self.ref.at[pl.ds(start + self.offset, count)]


def all_rows(refs):
    return tuple(Rows(ref, -n if n < STEPS else 0) for n, ref in enumerate(refs))


class Dims:
    def __init__(self, levels, bits, gx):
        self.q = bits.shape[0]
        self.pl, self.rows, self.cols = levels.shape
        self.ct = self.cols // LANES
        self.rt = self.rows // SUB
        self.width = self.cols + LANES
        self.total_rows = self.rows * gx
        self.row_tiles = self.pl * self.ct
        self.per_corner = LANES // (2 * STEPS)
        self.per_edge = LANES // STEPS
        self.corner_v = -(-STEPS * self.pl // self.per_corner)
        self.corner_tiles = self.corner_v + 1
        self.edge_v = -(-self.rows * self.pl // self.per_edge)
        self.edge_tiles = self.edge_v + -(-self.rows // self.per_edge)
        self.plan = {
            "ua": ((1, 2), (), False),
            "ub": ((3, 4), (1, 2, 3), True),
            "da": ((1, 2), (1, 2), True),
            "db": ((3,), (), False),
            "dc": ((4,), (3,), False),
        }

    def tiles(self, name):
        v_rows, o_rows, corners = self.plan[name]
        return len(v_rows) * self.row_tiles + len(o_rows) * self.ct + corners * self.corner_tiles

    def halo(self, name, k):
        return STEPS - k if name[0] == "u" else STEPS + self.rows - 1 + k

    def source(self, name, k):
        return STEPS + self.rows - k if name[0] == "u" else STEPS - 1 + k


def lanes_of(t):
    return slice(t * LANES, (t + 1) * LANES)


def to_spin(bits):
    return (2 * bits - 1).astype(F32)


def first_kernel(d, _, __, bits_ref, out_ref, scratch, sem):
    size = d.ct * SUB
    copies = [
        pltpu.make_async_copy(
            bits_ref.at[:, p, pl.ds((d.rt - 1) * size, size)], scratch.at[p], sem.at[p]
        )
        for p in range(d.pl)
    ]
    for copy in copies:
        copy.start()
    for p, copy in enumerate(copies):
        copy.wait()
        flat = scratch.at[p].reshape(d.q * size, LANES)
        for i, k in enumerate(d.plan["ua"][0]):
            for t in range(d.ct):
                bits = flat[pl.ds(t * SUB + SUB - k, d.q, stride=size), :]
                out_ref[i * d.row_tiles + p * d.ct + t] = to_spin(bits)


def fill_kernel(d, row_ref, bits_ref, levels_ref, v_ref, ons_ref, *refs):
    sends = dict(zip(("ub", "da", "db", "dc"), refs))
    right_ref, left_ref, scratch, lscratch, sem = refs[4:]
    lcopy = pltpu.make_async_copy(levels_ref, lscratch, sem.at[d.pl])
    copies = [
        pltpu.make_async_copy(bits_ref.at[:, p], scratch.at[p], sem.at[p]) for p in range(d.pl)
    ]
    lcopy.start()
    for copy in copies:
        copy.start()
    lcopy.wait()
    first_row = row_ref[0]
    for r in range(d.rt):
        for t in range(d.ct):
            level = lscratch[:, pl.ds((r * d.ct + t) * SUB, SUB), :].astype(F32)
            sub = lax.broadcasted_iota(jnp.int32, level.shape, 1)
            index = (first_row + r * SUB + sub).astype(F32)
            field = field_strength * ((index + 0.5) / d.total_rows - 0.5)
            onsite = disorder_width * (level / (LEVELS - 1) - 0.5) + field
            onsite = jnp.swapaxes(onsite * HOP, 0, 1)
            for i in range(SUB):
                ons_ref[STEPS + r * SUB + i, :, lanes_of(t)] = onsite[i]
    for p, copy in enumerate(copies):
        copy.wait()

        def block(r, _, p=p):
            for t in range(d.ct):
                start = pl.multiple_of((r * d.ct + t) * SUB, SUB)
                spins = jnp.swapaxes(to_spin(scratch[p, :, pl.ds(start, SUB), :]), 0, 1)
                v_ref[pl.ds(STEPS + r * SUB, SUB), p, :, lanes_of(t)] = spins
            return 0

        lax.fori_loop(0, d.rt, block, 0)
    lane = lax.broadcasted_iota(jnp.int32, (SUB, LANES), 1)
    low, high = lane < STEPS, lane >= LANES - STEPS

    def pack(items, ref, base, low_side):
        for at in range(0, len(items), d.per_edge):
            total = None
            for g, item in enumerate(items[at : at + d.per_edge]):
                tile = jnp.where(low if low_side else high, item(), 0.0)
                moved = pltpu.roll(tile, (STEPS * g + (0 if low_side else STEPS)) % LANES, 1)
                total = moved if total is None else total + moved
            ref[base + at // d.per_edge] = total

    for ref, t, low_side in ((right_ref, d.ct - 1, False), (left_ref, 0, True)):
        at = lanes_of(t)
        spins = [
            lambda r=r, p=p: v_ref[STEPS + r, p, :, at] for r in range(d.rows) for p in range(d.pl)
        ]
        pack(spins, ref, 0, low_side)
        onsite = [lambda r=r: ons_ref[STEPS + r, :, at] for r in range(d.rows)]
        pack(onsite, ref, d.edge_v, low_side)
    for name, ref in sends.items():
        v_rows, o_rows, _ = d.plan[name]
        for i, k in enumerate(v_rows):
            for p in range(d.pl):
                for t in range(d.ct):
                    ref[i * d.row_tiles + p * d.ct + t] = v_ref[d.source(name, k), p, :, lanes_of(t)]
        base = len(v_rows) * d.row_tiles
        for i, k in enumerate(o_rows):
            for t in range(d.ct):
                ref[base + i * d.ct + t] = ons_ref[d.source(name, k), :, lanes_of(t)]


def side_kernel(d, before_ref, after_ref, v_in, o_in, ub_in, da_in, v_ref, ons_ref, ub_ref, da_ref):
    lane = lax.broadcasted_iota(jnp.int32, (SUB, LANES), 1)
    low, high = lane < STEPS, lane >= LANES - STEPS

    def side(base, i):
        tile, g = base + i // d.per_edge, i % d.per_edge
        after = pltpu.roll(after_ref[tile], (-STEPS * g) % LANES, 1)
        before = pltpu.roll(before_ref[tile], (LANES - STEPS - STEPS * g) % LANES, 1)
        return jnp.where(low, after, jnp.where(high, before, 0.0))

    at = slice(d.cols, d.width)
    for r in range(d.rows):
        for p in range(d.pl):
            v_ref[STEPS + r, p, :, at] = side(0, r * d.pl + p)
        ons_ref[STEPS + r, :, at] = side(d.edge_v, r)
    for name, ref in (("ub", ub_ref), ("da", da_ref)):
        spins = [
            v_ref[d.source(name, k), p, :, at] for k in range(1, STEPS + 1) for p in range(d.pl)
        ]
        onsite = [ons_ref[d.source(name, k), :, at] for k in range(1, STEPS)]
        base = d.tiles(name) - d.corner_tiles
        for items, first in ((spins, base), (onsite, base + d.corner_v)):
            for start in range(0, len(items), d.per_corner):
                total = None
                for g, item in enumerate(items[start : start + d.per_corner]):
                    moved = pltpu.roll(item, (STEPS + 2 * STEPS * g) % LANES, 1)
                    total = moved if total is None else total + moved
                ref[first + start // d.per_corner] = total


def install(d, name, ref, v_ref, ons_ref):
    v_rows, o_rows, corners = d.plan[name]
    for i, k in enumerate(v_rows):
        for p in range(d.pl):
            for t in range(d.ct):
                v_ref[d.halo(name, k), p, :, lanes_of(t)] = ref[i * d.row_tiles + p * d.ct + t]
    base = len(v_rows) * d.row_tiles
    for i, k in enumerate(o_rows):
        for t in range(d.ct):
            ons_ref[d.halo(name, k), :, lanes_of(t)] = ref[base + i * d.ct + t]
    if not corners:
        return
    lane = lax.broadcasted_iota(jnp.int32, (SUB, LANES), 1)
    edge = (lane < STEPS) | (lane >= LANES - STEPS)
    at = slice(d.cols, d.width)

    def corner(first, i):
        tile, g = first + i // d.per_corner, i % d.per_corner
        moved = pltpu.roll(ref[tile], (-(STEPS + 2 * STEPS * g)) % LANES, 1)
        return jnp.where(edge, moved, 0.0)

    base = d.tiles(name) - d.corner_tiles
    for k in range(1, STEPS + 1):
        for p in range(d.pl):
            v_ref[d.halo(name, k), p, :, at] = corner(base, (k - 1) * d.pl + p)
        if k < STEPS:
            ons_ref[d.halo(name, k), :, at] = corner(base + d.corner_v, k - 1)


def row_values(d, n, at, v, ons, one_sided=False):
    source = v[n - 1]
    values = []
    for p in range(d.pl):
        x = source[at, p]
        beside = source[at - 1, p]
        if not one_sided:
            beside = beside + source[at + 1, p]
        beside = beside + pltpu.roll(x, 1, 1) + pltpu.roll(x, d.width - 1, 1)
        if p + 1 < d.pl:
            beside = beside + source[at, p + 1]
        if p > 0:
            beside = beside + source[at, p - 1]
        value = ons[at, pl.ds(p, SUB, stride=0), :] * x - HOP * beside
        values.append(0.5 * value if n == 1 else value - v[n - 2][at, p])
    return values


def one_row(d, n, at, v, ons):
    for p, value in enumerate(row_values(d, n, at, v, ons)):
        if n < STEPS:
            v[n][at, p] = value
        else:
            v[n][at - STEPS, p, :, : d.cols] = value[:, : d.cols]


def split_pair(x):
    high = x.astype(jnp.bfloat16).astype(F32)
    return high, x - high


def gram_row(d, at, v, last):
    total = None
    for p in range(d.pl):
        spin = v[0][at, p, :, : d.cols]
        halves = [split_pair(v[m][at, p, :, : d.cols]) for m in range(1, STEPS)]
        halves.append(split_pair(last(p)))
        right = [spin, spin]
        for pair in halves:
            right += list(pair)
        third = halves[STEPS - 2]
        left = [spin, third[0], third[1], third[1]]
        right = jnp.concatenate(right, 0).astype(jnp.bfloat16)
        left = jnp.concatenate(left, 0).astype(jnp.bfloat16)
        part = lax.dot_general(
            left, right, (((1,), (1,)), ((), ())), preferred_element_type=F32
        )
        total = part if total is None else total + part
    return total[: 3 * d.q]


def gram_shape(d):
    return (3 * d.q, LANES)


def add_gram(gram_ref, part):
    gram_ref[:, : part.shape[1]] += part


def packed_gram(d, gram):
    q = d.q
    zero, high, low = gram[:q], gram[q : 2 * q], gram[2 * q :]
    lane = lax.broadcasted_iota(jnp.int32, zero.shape, 1)
    with_zero = jnp.where(lane < q, zero, zero + pltpu.roll(zero, LANES - q, 1))
    with_third = high + pltpu.roll(high, LANES - q, 1) + low
    return jnp.where(lane % (2 * q) < q, with_zero, pltpu.roll(with_third, q, 1))


def interior_kernel(d, v_ref, ons, *refs):
    v, gram_ref = all_rows((v_ref,) + refs[:STEPS]), refs[STEPS]
    gram_ref[...] = jnp.zeros(gram_ref.shape, F32)
    for n in range(1, STEPS + 1):

        def step(row, _, n=n):
            at = row + STEPS
            one_row(d, n, at, v, ons)
            if n == STEPS:
                add_gram(gram_ref, gram_row(d, at, v, lambda p: v[n][row, p, :, : d.cols]))
            return 0

        lax.fori_loop(n, d.rows - n, step, 0)


def edge_rows(d):
    top = STEPS + d.rows - 1
    return [(n, top + STEPS - 1 - n - i) for n in range(STEPS - 1) for i in range(2)]


def wave_kernel(d, names, waves, *refs):
    recv = refs[: len(names)]
    refs = refs[len(names) + STEPS + 3 :]
    v = all_rows(refs[: STEPS + 1])
    ons, gram_ref, *extra = refs[STEPS + 1 :]
    for name, ref in zip(names, recv):
        install(d, name, ref, v[0], ons)

    def gram(at, last=None):
        part = gram_row(d, at, v, last or (lambda p: v[STEPS][at - STEPS, p, :, : d.cols]))
        add_gram(gram_ref, part)

    for side, k in waves:
        at_of = lambda n: STEPS + n - k if side == "u" else STEPS + d.rows - 1 - (n - k)
        for n in range(1, STEPS):
            one_row(d, n, at_of(n), v, ons)
        at = at_of(STEPS)
        if k < STEPS:
            one_row(d, STEPS, at, v, ons)
            gram(at)
        elif side == "u":
            one_row(d, STEPS, at, v, ons)
            gram(at, lambda p: v[STEPS][0, p, :, : d.cols] - HOP * v[STEPS - 1][at - 1, p, :, : d.cols])
    if ("d", STEPS - 1) in waves:
        at = STEPS + d.rows - 1
        for p, value in enumerate(row_values(d, STEPS, at, v, ons, one_sided=True)):
            v[STEPS][d.rows - 1, p, :, : d.cols] = value[:, : d.cols]
        gram(at)
    if ("u", STEPS) in waves:
        flush(d, v[STEPS], *extra)
    if ("d", STEPS - 2) in waves:
        top_ref, sem = extra
        done = d.rows - 2 - (d.rt - 1) * SUB
        copy = pltpu.make_async_copy(
            v[STEPS].rows((d.rt - 1) * SUB, done).at[:, :, :, pl.ds(0, d.cols)],
            top_ref.at[pl.ds(0, done)], sem,
        )
        copy.start()
        copy.wait()
    if ("d", STEPS - 1) in waves:
        edge_ref, eons_ref, tail_ref, packed_ref = extra
        for i, (n, at) in enumerate(edge_rows(d)):
            edge_ref[i] = v[n][at]
        for k in range(1, STEPS - 1):
            eons_ref[k - 1] = ons[d.halo("dc", k)]
        for i in range(2):
            tail_ref[i] = v[STEPS][d.rows - 2 + i, :, :, : d.cols]
        packed_ref[...] = packed_gram(d, gram_ref[...])


def transpose_tiles(d, r, p, rows, stage):
    for t in range(d.ct):
        tile = rows[:, :, lanes_of(t)]
        stage[p, :, pl.ds((r * d.ct + t) * SUB, SUB), :] = jnp.swapaxes(tile, 0, 1)


def flush(d, v4, out_ref, stage, sem):
    size = (d.rt - 1) * d.ct * SUB
    copies = []
    for p in range(d.pl):
        for r in range(d.rt - 1):
            transpose_tiles(d, r, p, v4.rows(r * SUB, SUB)[:, p], stage)
        copies.append(
            pltpu.make_async_copy(stage.at[p], out_ref.at[:, p, pl.ds(0, size)], sem.at[p])
        )
        copies[-1].start()
    for copy in copies:
        copy.wait()


def last_kernel(
    d, dc_ref, edge_ref, eons_ref, tail_ref, top_ref, _, out_ref, work, wons, rows, stage, sem, osem
):
    loads = [
        pltpu.make_async_copy(top_ref.at[pl.ds(0, SUB - 2), p], rows.at[p, pl.ds(0, SUB - 2)], sem.at[p])
        for p in range(d.pl)
    ]
    for load in loads:
        load.start()
    for n in range(STEPS - 1):
        for i in range(2):
            work[3 * n + 1 + i] = edge_ref[2 * n + i]
    for i in range(d.row_tiles):
        p, t = i // d.ct, i % d.ct
        work[0, p, :, lanes_of(t)] = dc_ref[i]
    for t in range(d.ct):
        wons[0, :, lanes_of(t)] = dc_ref[d.row_tiles + t]
    work[0, :, :, d.cols :] = jnp.zeros((d.pl, d.q, LANES), F32)
    wons[0, :, d.cols :] = jnp.zeros((d.pl, LANES), F32)
    for k in range(STEPS - 2):
        wons[STEPS - 2 - k] = eons_ref[k]
    for n in range(1, STEPS):
        base = 3 * (n - 1)
        for p in range(d.pl):
            x = work[base + 1, p]
            beside = work[base, p] + work[base + 2, p]
            beside = beside + pltpu.roll(x, 1, 1) + pltpu.roll(x, d.width - 1, 1)
            if p + 1 < d.pl:
                beside = beside + work[base + 1, p + 1]
            if p > 0:
                beside = beside + work[base + 1, p - 1]
            value = wons[n - 1, pl.ds(p, SUB, stride=0), :] * x - HOP * beside
            work[3 * n, p] = 0.5 * value if n == 1 else value - work[base - 1, p]
    copies = []
    size = d.ct * SUB
    for p in range(d.pl):
        rows[p, SUB - 2] = tail_ref[0, p]
        rows[p, SUB - 1] = tail_ref[1, p] - HOP * work[3 * STEPS - 3, p, :, : d.cols]
        loads[p].wait()
        transpose_tiles(d, 0, p, rows[p], stage)
        copies.append(pltpu.make_async_copy(
            stage.at[p], out_ref.at[:, p, pl.ds((d.rt - 1) * size, size)], osem.at[p]
        ))
        copies[-1].start()
    for copy in copies:
        copy.wait()


def green_kernel(d, sites, tables_ref, packed_ref, out_ref):
    q = d.q
    rest = packed_ref[...]
    parts = []
    for _ in range(3):
        parts.append(rest.astype(jnp.bfloat16).astype(F32))
        rest = rest - parts[-1]
    left = jnp.concatenate(parts + [jnp.zeros_like(rest)], 0).astype(jnp.bfloat16)
    column = lax.broadcasted_iota(jnp.int32, (LANES, LANES), 0)
    lane = lax.broadcasted_iota(jnp.int32, (LANES, LANES), 1)
    sub = lax.broadcasted_iota(jnp.int32, (q, LANES), 0)
    out_lane = lax.broadcasted_iota(jnp.int32, (q, LANES), 1)
    major, minor = lane // q, lane % q
    used = lane < q * q
    blocks = [2 * m for m in range(STEPS)] + [2 * m + 1 for m in range(1, STEPS + 1)]
    picks = []
    for block in blocks:
        for index in (minor, major):
            hit = (column == block * q + index) & used
            picks.append(jnp.where(hit, 1.0, 0.0).astype(jnp.bfloat16))
    wide = jnp.dot(left, jnp.concatenate(picks, 1), preferred_element_type=F32)
    wide = wide[:q] + wide[q : 2 * q] + wide[2 * q : 3 * q]
    straight, turned = sub == out_lane // q, sub == out_lane % q
    flat = []
    for i in range(len(blocks)):
        one = jnp.where(straight, wide[:, lanes_of(2 * i)], 0.0)
        two = jnp.where(turned, wide[:, lanes_of(2 * i + 1)], 0.0)
        flat.append(jnp.sum(one + two, 0, keepdims=True) * (0.5 / sites))
    moments = flat[:STEPS]
    for m, base in ((0, 2), (1, 1), (2, 0), (3, 1)):
        moments.append(2.0 * flat[STEPS + m] - moments[base])
    moments = jnp.concatenate(moments, 0)
    total = lax.dot_general(
        moments, tables_ref[...], (((0,), (0,)), ((), ())),
        precision=lax.Precision.HIGHEST, preferred_element_type=F32,
    )
    energies = total.shape[1] // 2
    for part in range(2):
        out_ref[part] = total[: q * q, part * energies : (part + 1) * energies]


def jackson_weights(count):
    total = count + 1.0
    values = []
    for order in range(count):
        damping = (
            (count - order + 1.0) * math.cos(math.pi * order / total)
            + math.sin(math.pi * order / total) / math.tan(math.pi / total)
        ) / total
        values.append(damping if order == 0 else 2.0 * damping)
    return jnp.asarray(values, dtype=F32)


def energy_tables(energy_index, count, total_energies):
    phase = math.pi * (energy_index.astype(F32) + 0.5) / total_energies
    theta = jnp.arccos(energy_edge * jnp.cos(phase))
    orders = jnp.arange(count).astype(F32)
    weights = jackson_weights(count)
    angles = orders[:, None] * theta[None, :]
    denominator = jnp.sin(theta)[None, :]
    real_part = -weights[:, None] * jnp.sin(angles) / denominator
    imag_part = -weights[:, None] * jnp.cos(angles) / denominator
    return jnp.concatenate([real_part, imag_part], 1)


def add_over(value, axis):
    peers = lax.axis_size(axis)
    if peers & (peers - 1):
        return lax.psum(value, axis)
    if peers == 4:
        others = [lax.ppermute(value, axis, [(i, i ^ s) for i in range(peers)]) for s in (1, 2, 3)]
        return (value + others[0]) + (others[1] + others[2])
    shift = 1
    while shift < peers:
        value = value + lax.ppermute(value, axis, [(i, i ^ shift) for i in range(peers)])
        shift *= 2
    return value


VMEM = pl.BlockSpec(memory_space=pltpu.VMEM)
SMEM = pl.BlockSpec(memory_space=pltpu.SMEM)
HBM = pl.BlockSpec(memory_space=pltpu.MemorySpace.HBM)


def params(mib):
    return pltpu.CompilerParams(vmem_limit_bytes=mib * 2**20)


def send(array, axis, step):
    peers = lax.axis_size(axis)
    return lax.ppermute(array, axis, [(i, (i + step) % peers) for i in range(peers)])


def on_device(levels, probe_bits):
    count_gx = lax.axis_size("gx")
    count_gy = lax.axis_size("gy")
    d = Dims(levels, probe_bits, count_gx)
    sites = d.pl * d.total_rows * d.cols * count_gy
    first_row = (lax.axis_index("gx") * d.rows).astype(jnp.int32).reshape(1)
    in_hbm = lambda x: pltpu.with_memory_space_constraint(x, pltpu.MemorySpace.HBM)
    per_device = NE // (count_gx * count_gy)
    first_energy = (lax.axis_index("gx") * count_gy + lax.axis_index("gy")) * per_device
    first_energy = first_energy.astype(jnp.int32).reshape(1)
    bits = tile_view(probe_bits, (d.q, d.pl))
    levels = in_hbm(tile_view(levels, (d.pl,)))
    dma = pltpu.SemaphoreType.DMA
    padded = d.rows + 2 * STEPS
    vectors = [pltpu.VMEM((padded - 2 * n, d.pl, d.q, d.width), F32) for n in range(STEPS)]
    last = pltpu.VMEM((d.rows, d.pl, d.q, d.cols), F32)
    onsite = pltpu.VMEM((padded, d.pl, d.width), F32)
    gram_type = pltpu.VMEM(gram_shape(d), F32)
    tiles = lambda n: pltpu.VMEM((n, SUB, LANES), F32)

    ua = pl.pallas_call(
        functools.partial(first_kernel, d),
        out_shape=tiles(d.tiles("ua")), in_specs=[SMEM, SMEM, HBM], out_specs=VMEM,
        scratch_shapes=[pltpu.VMEM((d.pl, d.q, d.ct * SUB, LANES), jnp.int32), dma((d.pl,))],
        compiler_params=params(4), name="first",
    )(first_row, first_energy, in_hbm(bits))
    ua = send(ua, "gx", 1)
    names = ("ub", "da", "db", "dc")
    v0, ons, *sends, right, left = pl.pallas_call(
        functools.partial(fill_kernel, d),
        out_shape=[vectors[0], onsite] + [tiles(d.tiles(name)) for name in names]
        + [tiles(d.edge_tiles)] * 2,
        in_specs=[SMEM, HBM, HBM], out_specs=[VMEM] * 8,
        scratch_shapes=[
            pltpu.VMEM((d.pl, d.q) + bits.shape[2:], jnp.int32), pltpu.VMEM(levels.shape, jnp.int32),
            dma((d.pl + 1,)),
        ],
        compiler_params=params(6), name="fill",
    )(first_row, in_hbm(bits), levels)
    ub, da, db, dc = sends
    before = send(right, "gy", 1)
    after = send(left, "gy", -1)
    v0, ons, ub, da = pl.pallas_call(
        functools.partial(side_kernel, d),
        out_shape=[vectors[0], onsite, tiles(d.tiles("ub")), tiles(d.tiles("da"))],
        in_specs=[VMEM] * 6, out_specs=[VMEM] * 4,
        input_output_aliases={2: 0, 3: 1, 4: 2, 5: 3},
        compiler_params=params(2), name="side",
    )(before, after, v0, ons, ub, da)
    ub = send(ub, "gx", 1)
    da = send(da, "gx", -1)
    db = send(db, "gx", -1)
    dc = send(dc, "gx", -1)
    *rest, gram = pl.pallas_call(
        functools.partial(interior_kernel, d),
        out_shape=vectors[1:] + [last, gram_type], in_specs=[VMEM] * 2, out_specs=[VMEM] * (STEPS + 1),
        compiler_params=params(3), name="interior",
    )(v0, ons)
    kept = [v0] + rest + [ons, gram]
    kinds = vectors + [last, onsite, gram_type]

    def wave(received, names, waves, kept, extra=(), specs=(), scratch=()):
        return pl.pallas_call(
            functools.partial(wave_kernel, d, names, waves),
            out_shape=kinds + list(extra), in_specs=[VMEM] * (len(names) + len(kept)),
            out_specs=[VMEM] * len(kept) + list(specs), scratch_shapes=list(scratch),
            input_output_aliases={len(names) + i: i for i in range(len(kept))},
            compiler_params=params(4),
        )(*received, *kept)

    every = tuple(("u", k) for k in range(1, STEPS + 1))
    stage_rows = (d.rt - 1) * d.ct * SUB
    *kept, lower = wave(
        [ua, ub], ("ua", "ub"), every, kept, [pltpu.HBM(bits.shape, F32)], [HBM],
        [pltpu.VMEM((d.pl, d.q, stage_rows, LANES), F32), dma((d.pl,))],
    )
    block = (SUB, d.pl, d.q, d.cols)
    *kept, top = wave(
        [da], ("da",), (("d", 1), ("d", 2)), kept,
        [pltpu.HBM(block, F32)], [HBM], [dma],
    )
    extra = [
        pltpu.VMEM((2 * (STEPS - 1), d.pl, d.q, d.width), F32),
        pltpu.VMEM((STEPS - 2, d.pl, d.width), F32),
        pltpu.VMEM((2,) + block[1:], F32),
        pltpu.VMEM((d.q, LANES), F32),
    ]
    *_, edge, edge_ons, tail, gram = wave([db], ("db",), (("d", 3),), kept, extra, [VMEM] * 4)
    last_vector = pl.pallas_call(
        functools.partial(last_kernel, d),
        out_shape=jax.ShapeDtypeStruct(bits.shape, F32),
        in_specs=[VMEM] * 4 + [HBM] * 2, out_specs=HBM,
        scratch_shapes=[
            pltpu.VMEM((3 * STEPS - 2, d.pl, d.q, d.width), F32),
            pltpu.VMEM((STEPS - 1, d.pl, d.width), F32),
            pltpu.VMEM((d.pl, SUB, d.q, d.cols), F32),
            pltpu.VMEM((d.pl, d.q, d.ct * SUB, LANES), F32), dma((d.pl,)), dma((d.pl,)),
        ],
        input_output_aliases={5: 0},
        compiler_params=params(9), name="last",
    )(dc, edge, edge_ons, tail, top, lower)
    last_vector = untile_view(last_vector, probe_bits.shape)

    gram = add_over(add_over(gram, "gy"), "gx")
    tables = energy_tables(first_energy + jnp.arange(per_device), NMOM, NE)
    green = pl.pallas_call(
        functools.partial(green_kernel, d, sites),
        out_shape=jax.ShapeDtypeStruct((2, d.q * d.q, per_device), F32),
        in_specs=[VMEM] * 2, out_specs=VMEM, compiler_params=params(2), name="green",
    )(tables, gram)
    return green.transpose(0, 2, 1), last_vector


def solution(mesh):
    placed = (P(None, "gx", "gy"), P(None, None, "gx", "gy"))
    return jax.shard_map(
        on_device,
        mesh=mesh,
        in_specs=placed,
        out_specs=(P(None, ("gx", "gy"), None), P(None, None, "gx", "gy")),
        check_vma=False,
    )
```

```python
import functools
import math

import jax
import jax.numpy as jnp
from jax import lax
from jax.experimental import pallas as pl
from jax.experimental.pallas import tpu as pltpu
from jax.sharding import PartitionSpec as P


STEPS = 4
LEVELS = 8
NE = 8192
NMOM = 2 * STEPS
LANES = 128
SUB = 8

disorder_width = 4.0
field_strength = 3.0
spectral_scale = 10.0
energy_edge = 0.9

F32 = jnp.float32


HOP = 2.0 / spectral_scale


def tile_view(array, lead):
    _, cols = array.shape[-2:]
    split = array.reshape(lead + (-1, SUB, cols // LANES, LANES))
    n = len(lead)
    return split.transpose(*range(n + 1), n + 2, n + 1, n + 3).reshape(lead + (-1, LANES))


def untile_view(view, shape):
    rows, cols = shape[-2:]
    split = view.reshape(-1, rows // SUB, cols // LANES, SUB, LANES)
    return split.transpose(0, 1, 3, 2, 4).reshape(shape)


class Rows:
    def __init__(self, ref, offset):
        self.ref, self.offset = ref, offset

    def __getitem__(self, index):
        if isinstance(index, tuple):
            return self.ref[(index[0] + self.offset,) + index[1:]]
        return self.ref[index + self.offset]

    def __setitem__(self, index, value):
        self.ref[(index[0] + self.offset,) + index[1:]] = value

    def rows(self, start, count):
        return self.ref.at[pl.ds(start + self.offset, count)]


def all_rows(refs):
    return tuple(Rows(ref, -n if n < STEPS else 0) for n, ref in enumerate(refs))


class Dims:
    def __init__(self, levels, bits, gx):
        self.q = bits.shape[0]
        self.pl, self.rows, self.cols = levels.shape
        self.ct = self.cols // LANES
        self.rt = self.rows // SUB
        self.width = self.cols + LANES
        self.total_rows = self.rows * gx
        self.row_tiles = self.pl * self.ct
        self.per_corner = LANES // (2 * STEPS)
        self.per_edge = LANES // STEPS
        self.edge_v = -(-self.rows * self.pl // self.per_edge)
        self.edge_tiles = self.edge_v + -(-self.rows // self.per_edge)
        self.plan = {
            "ua": (((0, 1), (0, 2)), 0, ()),
            "ub": (((1, 2), (2, 2)), 1, ((0, 1), (0, 2), (1, 2))),
            "da": (((0, 1), (0, 2)), 1, ((0, 1), (0, 2))),
            "db": (((1, 2),), 0, ((1, 2),)),
            "dc": (((2, 2),), 0, ()),
        }

    def places(self, name):
        rows, onsite, corners = self.plan[name]
        first = len(rows) * self.row_tiles
        second = first + onsite * self.ct
        third = second - (-len(corners) * self.pl // self.per_corner)
        return first, second, third, third + (onsite if corners else 0)

    def tiles(self, name):
        return self.places(name)[-1]

    def halo(self, name, k):
        return STEPS - k if name[0] == "u" else STEPS + self.rows - 1 + k

    def source(self, name, k):
        return STEPS + self.rows - k if name[0] == "u" else STEPS - 1 + k


def lanes_of(t):
    return slice(t * LANES, (t + 1) * LANES)


def to_spin(bits):
    return (2 * bits - 1).astype(F32)


def first_kernel(d, __, ___, bits_ref, out_ref, scratch, sem):
    size = d.ct * SUB
    copies = [
        pltpu.make_async_copy(
            bits_ref.at[:, p, pl.ds((d.rt - 1) * size, size)], scratch.at[p], sem.at[p]
        )
        for p in range(d.pl)
    ]
    for copy in copies:
        copy.start()
    for p, copy in enumerate(copies):
        copy.wait()
        flat = scratch.at[p].reshape(d.q * size, LANES)
        for i, (_, k) in enumerate(d.plan["ua"][0]):
            for t in range(d.ct):
                bits = flat[pl.ds(t * SUB + SUB - k, d.q, stride=size), :]
                out_ref[i * d.row_tiles + p * d.ct + t] = to_spin(bits)


def fill_kernel(
    d, row_ref, bits_ref, levels_ref, v_ref, ons_ref, da_ref, right_ref, left_ref, scratch, lscratch, sem
):
    lcopy = pltpu.make_async_copy(levels_ref, lscratch, sem.at[d.pl])
    copies = [
        pltpu.make_async_copy(bits_ref.at[:, p], scratch.at[p], sem.at[p]) for p in range(d.pl)
    ]
    lcopy.start()
    for copy in copies:
        copy.start()
    lcopy.wait()
    first_row = row_ref[0]
    for r in range(d.rt):
        for t in range(d.ct):
            level = lscratch[:, pl.ds((r * d.ct + t) * SUB, SUB), :].astype(F32)
            sub = lax.broadcasted_iota(jnp.int32, level.shape, 1)
            index = (first_row + r * SUB + sub).astype(F32)
            field = field_strength * ((index + 0.5) / d.total_rows - 0.5)
            onsite = disorder_width * (level / (LEVELS - 1) - 0.5) + field
            onsite = jnp.swapaxes(onsite * HOP, 0, 1)
            for i in range(SUB):
                ons_ref[STEPS + r * SUB + i, :, lanes_of(t)] = onsite[i]
    for p, copy in enumerate(copies):
        copy.wait()

        def block(r, _, p=p):
            for t in range(d.ct):
                start = pl.multiple_of((r * d.ct + t) * SUB, SUB)
                spins = jnp.swapaxes(to_spin(scratch[p, :, pl.ds(start, SUB), :]), 0, 1)
                v_ref[pl.ds(STEPS + r * SUB, SUB), p, :, lanes_of(t)] = spins
            return 0

        lax.fori_loop(0, d.rt, block, 0)
    lane = lax.broadcasted_iota(jnp.int32, (SUB, LANES), 1)
    low, high = lane < STEPS, lane >= LANES - STEPS

    def pack(items, ref, base, low_side):
        for at in range(0, len(items), d.per_edge):
            total = None
            for g, item in enumerate(items[at : at + d.per_edge]):
                tile = jnp.where(low if low_side else high, item(), 0.0)
                moved = pltpu.roll(tile, (STEPS * g + (0 if low_side else STEPS)) % LANES, 1)
                total = moved if total is None else total + moved
            ref[base + at // d.per_edge] = total

    for ref, t, low_side in ((right_ref, d.ct - 1, False), (left_ref, 0, True)):
        at = lanes_of(t)
        spins = [
            lambda r=r, p=p: v_ref[STEPS + r, p, :, at] for r in range(d.rows) for p in range(d.pl)
        ]
        pack(spins, ref, 0, low_side)
        onsite = [lambda r=r: ons_ref[STEPS + r, :, at] for r in range(d.rows)]
        pack(onsite, ref, d.edge_v, low_side)
    put_rows(d, "da", da_ref, {0: Rows(v_ref, 0)}, ons_ref)


def put_rows(d, name, ref, v, ons_ref):
    rows, onsite, _ = d.plan[name]
    for i, (n, k) in enumerate(rows):
        if n in v:
            for p in range(d.pl):
                for t in range(d.ct):
                    ref[i * d.row_tiles + p * d.ct + t] = v[n][d.source(name, k), p, :, lanes_of(t)]
    if onsite:
        for t in range(d.ct):
            ref[d.places(name)[0] + t] = ons_ref[d.source(name, 1), :, lanes_of(t)]


def side_kernel(
    d, before_ref, after_ref, v_in, o_in, da_in, v_ref, ons_ref, da_ref, ub_ref, db_ref, dc_ref, work
):
    lane = lax.broadcasted_iota(jnp.int32, (SUB, LANES), 1)
    low, high = lane < STEPS, lane >= LANES - STEPS

    def side(base, i):
        tile, g = base + i // d.per_edge, i % d.per_edge
        after = pltpu.roll(after_ref[tile], (-STEPS * g) % LANES, 1)
        before = pltpu.roll(before_ref[tile], (LANES - STEPS - STEPS * g) % LANES, 1)
        return jnp.where(low, after, jnp.where(high, before, 0.0))

    at = slice(d.cols, d.width)
    for r in range(d.rows):
        for p in range(d.pl):
            v_ref[STEPS + r, p, :, at] = side(0, r * d.pl + p)
        ons_ref[STEPS + r, :, at] = side(d.edge_v, r)
    v0 = Rows(v_ref, 0)
    for letter, named in (("u", {"ub": ub_ref}), ("d", {"da": da_ref, "db": db_ref, "dc": dc_ref})):
        second, third = d.source(letter, 2), d.source(letter, 3)
        v = (v0, Rows(work, -min(second, third)))
        for row in (third, second):
            one_row(d, 1, row, v, ons_ref)
        part = Rows(work, 2 - second)
        for p, value in enumerate(row_values(d, 2, second, v, ons_ref, leave=2 * second - third)):
            part[second, p] = value
        v = {0: v0, 1: v[1], 2: part}
        for name, ref in named.items():
            if name != "da":
                put_rows(d, name, ref, v, ons_ref)
            _, onsite, corners = d.plan[name]
            _, start, onsite_at, _ = d.places(name)
            packs = [(start, [(v[n], d.source(name, k), p) for n, k in corners for p in range(d.pl)])]
            for start, items in packs:
                for base in range(0, len(items), d.per_corner):
                    total = None
                    for g, (rows, row, p) in enumerate(items[base : base + d.per_corner]):
                        tile = jnp.where(low | high, rows[row, p, :, at], 0.0)
                        moved = pltpu.roll(tile, (STEPS + 2 * STEPS * g) % LANES, 1)
                        total = moved if total is None else total + moved
                    ref[start + base // d.per_corner] = total
            if onsite:
                ref[onsite_at] = ons_ref[d.source(name, 1), :, at]


def install(d, name, ref, v, ons_ref):
    rows, onsite, corners = d.plan[name]
    first, second, third, _ = d.places(name)
    for i, (n, k) in enumerate(rows):
        for p in range(d.pl):
            for t in range(d.ct):
                v[n][d.halo(name, k), p, :, lanes_of(t)] = ref[i * d.row_tiles + p * d.ct + t]
            if n == 2:
                v[n][d.halo(name, k), p, :, d.cols :] = jnp.zeros((d.q, LANES), F32)
    at = slice(d.cols, d.width)
    if onsite:
        for t in range(d.ct):
            ons_ref[d.halo(name, 1), :, lanes_of(t)] = ref[first + t]
        ons_ref[d.halo(name, 1), :, at] = ref[third]
    lane = lax.broadcasted_iota(jnp.int32, (SUB, LANES), 1)
    edge = (lane < STEPS) | (lane >= LANES - STEPS)
    for i, (n, k) in enumerate(corners):
        for p in range(d.pl):
            j = i * d.pl + p
            tile, g = second + j // d.per_corner, j % d.per_corner
            moved = pltpu.roll(ref[tile], (-(STEPS + 2 * STEPS * g)) % LANES, 1)
            v[n][d.halo(name, k), p, :, at] = jnp.where(edge, moved, 0.0)


def complete(d, letter, v):
    for p in range(d.pl):
        far, near = d.halo(letter, 2), d.halo(letter, 1)
        v[2][far, p] = v[2][far, p] - HOP * v[1][near, p]


def row_values(d, n, at, v, ons, leave=None):
    source = v[n - 1]
    values = []
    for p in range(d.pl):
        x = source[at, p]
        near = [source[row, p] for row in (at + 1, at - 1) if row != leave]
        beside = near[0] if leave is not None else near[0] + near[1]
        beside = beside + pltpu.roll(x, 1, 1) + pltpu.roll(x, d.width - 1, 1)
        if p + 1 < d.pl:
            beside = beside + source[at, p + 1]
        if p > 0:
            beside = beside + source[at, p - 1]
        value = ons[at, pl.ds(p, SUB, stride=0), :] * x - HOP * beside
        values.append(0.5 * value if n == 1 else value - v[n - 2][at, p])
    return values


def one_row(d, n, at, v, ons):
    for p, value in enumerate(row_values(d, n, at, v, ons)):
        if n < STEPS:
            v[n][at, p] = value
        else:
            v[n][at - STEPS, p] = value[:, : d.cols]


def split_pair(x):
    high = x.astype(jnp.bfloat16).astype(F32)
    return high, x - high


def gram_row(d, at, v, last):
    total = None
    for p in range(d.pl):
        spin = v[0][at, p, :, : d.cols]
        halves = [split_pair(v[m][at, p, :, : d.cols]) for m in range(1, STEPS)]
        halves.append(split_pair(last(p)))
        right = [spin, spin]
        for pair in halves:
            right += list(pair)
        third = halves[STEPS - 2]
        left = [spin, third[0], third[1], third[1]]
        right = jnp.concatenate(right, 0).astype(jnp.bfloat16)
        left = jnp.concatenate(left, 0).astype(jnp.bfloat16)
        part = lax.dot_general(
            left, right, (((1,), (1,)), ((), ())), preferred_element_type=F32
        )
        total = part if total is None else total + part
    return total[: 3 * d.q]


def gram_shape(d):
    return (3 * d.q, LANES)


def add_gram(gram_ref, part):
    gram_ref[:, : part.shape[1]] += part


def packed_gram(d, gram):
    q = d.q
    zero, high, low = gram[:q], gram[q : 2 * q], gram[2 * q :]
    lane = lax.broadcasted_iota(jnp.int32, zero.shape, 1)
    with_zero = jnp.where(lane < q, zero, zero + pltpu.roll(zero, LANES - q, 1))
    with_third = high + pltpu.roll(high, LANES - q, 1) + low
    return jnp.where(lane % (2 * q) < q, with_zero, pltpu.roll(with_third, q, 1))


def interior_kernel(d, v_ref, ons, *refs):
    v, gram_ref = all_rows((v_ref,) + refs[:STEPS]), refs[STEPS]
    gram_ref[...] = jnp.zeros(gram_ref.shape, F32)
    for n in range(1, STEPS + 1):

        def step(row, _, n=n):
            at = row + STEPS
            one_row(d, n, at, v, ons)
            if n == STEPS:
                add_gram(gram_ref, gram_row(d, at, v, lambda p: v[n][row, p]))
            return 0

        lax.fori_loop(n, d.rows - n, step, 0)


def wave_kernel(d, names, waves, *refs):
    recv = refs[: len(names)]
    refs = refs[len(names) + STEPS + 3 :]
    v = all_rows(refs[: STEPS + 1])
    ons, gram_ref, *extra = refs[STEPS + 1 :]
    for name, ref in zip(names, recv):
        install(d, name, ref, v, ons)

    def gram(at, last=None):
        part = gram_row(d, at, v, last or (lambda p: v[STEPS][at - STEPS, p]))
        add_gram(gram_ref, part)

    top = STEPS + d.rows - 1
    for side, k in waves:
        at_of = lambda n: STEPS + n - k if side == "u" else top - (n - k)
        if k == STEPS:
            complete(d, side, v)
        for n in range(max(1, k - 1), STEPS):
            one_row(d, n, at_of(n), v, ons)
        at = at_of(STEPS)
        if side == "u" or k < STEPS - 1:
            one_row(d, STEPS, at, v, ons)
            inner = HOP if side == "u" and k == STEPS else None
            gram(at, inner and (lambda p: v[STEPS][0, p] - inner * v[STEPS - 1][at - 1, p, :, : d.cols]))
    if ("u", STEPS) in waves:
        flush(d, v[STEPS], *extra)
    if ("d", STEPS - 2) in waves:
        for p, value in enumerate(row_values(d, STEPS, top - 1, v, ons, leave=top)):
            v[STEPS][d.rows - 2, p] = value[:, : d.cols]
        gram(top - 1)
    if ("d", STEPS - 1) in waves:
        for p, value in enumerate(row_values(d, STEPS, top, v, ons, leave=top + 1)):
            v[STEPS][d.rows - 1, p] = value[:, : d.cols]
        gram(top, lambda p: v[STEPS][d.rows - 1, p] - HOP * v[STEPS - 1][top - 1, p, :, : d.cols])
        extra[0][...] = packed_gram(d, gram_ref[...])


def transpose_tiles(d, r, p, rows, stage):
    for t in range(d.ct):
        tile = rows[:, :, lanes_of(t)]
        stage[p, :, pl.ds((r * d.ct + t) * SUB, SUB), :] = jnp.swapaxes(tile, 0, 1)


def flush(d, v4, out_ref, stage, sem):
    size = (d.rt - 1) * d.ct * SUB
    copies = []
    for p in range(d.pl):
        for r in range(d.rt - 1):
            transpose_tiles(d, r, p, v4.rows(r * SUB, SUB)[:, p], stage)
        copies.append(
            pltpu.make_async_copy(stage.at[p], out_ref.at[:, p, pl.ds(0, size)], sem.at[p])
        )
        copies[-1].start()
    for copy in copies:
        copy.wait()


def last_kernel(d, dc_ref, *refs):
    out_ref, *refs = refs[STEPS + 3 :]
    v, (ons, stage, sem) = all_rows(refs[: STEPS + 1]), refs[STEPS + 1 :]
    install(d, "dc", dc_ref, v, ons)
    complete(d, "d", v)
    top = STEPS + d.rows - 1
    one_row(d, STEPS - 1, top + 1, v, ons)
    copies = []
    size = d.ct * SUB
    for p in range(d.pl):
        for row in (d.rows - 2, d.rows - 1):
            above = v[STEPS - 1][row + STEPS + 1, p, :, : d.cols]
            v[STEPS][row, p] = v[STEPS][row, p] - HOP * above
        transpose_tiles(d, 0, p, v[STEPS].rows((d.rt - 1) * SUB, SUB)[:, p], stage)
        copies.append(pltpu.make_async_copy(
            stage.at[p], out_ref.at[:, p, pl.ds((d.rt - 1) * size, size)], sem.at[p]
        ))
        copies[-1].start()
    for copy in copies:
        copy.wait()


def moment_blocks():
    return [2 * m for m in range(STEPS)] + [2 * m + 1 for m in range(1, STEPS + 1)]


def pick_kernel(d, out_ref):
    column = lax.broadcasted_iota(jnp.int32, (LANES, LANES), 0)
    lane = lax.broadcasted_iota(jnp.int32, (LANES, LANES), 1)
    for i, block in enumerate(moment_blocks()):
        for turned, index in enumerate((lane % d.q, lane // d.q)):
            hit = (column == block * d.q + index) & (lane < d.q * d.q)
            out_ref[:, lanes_of(2 * i + turned)] = jnp.where(hit, 1.0, 0.0).astype(jnp.bfloat16)


def green_kernel(d, sites, tables_ref, picks_ref, packed_ref, out_ref):
    q = d.q
    rest = packed_ref[...]
    parts = []
    for _ in range(3):
        parts.append(rest.astype(jnp.bfloat16).astype(F32))
        rest = rest - parts[-1]
    left = jnp.concatenate(parts + [jnp.zeros_like(rest)], 0).astype(jnp.bfloat16)
    sub = lax.broadcasted_iota(jnp.int32, (q, LANES), 0)
    out_lane = lax.broadcasted_iota(jnp.int32, (q, LANES), 1)
    wide = jnp.dot(left, picks_ref[...], preferred_element_type=F32)
    wide = wide[:q] + wide[q : 2 * q] + wide[2 * q : 3 * q]
    straight, turned = sub == out_lane // q, sub == out_lane % q
    flat = []
    for i in range(len(moment_blocks())):
        one = jnp.where(straight, wide[:, lanes_of(2 * i)], 0.0)
        two = jnp.where(turned, wide[:, lanes_of(2 * i + 1)], 0.0)
        flat.append(jnp.sum(one + two, 0, keepdims=True) * (0.5 / sites))
    moments = flat[:STEPS]
    for m, base in ((0, 2), (1, 1), (2, 0), (3, 1)):
        moments.append(2.0 * flat[STEPS + m] - moments[base])
    high, low = split_pair(jnp.concatenate(moments, 0))
    weight, weight_low = split_pair(tables_ref[...])
    left = jnp.concatenate([high, high, low, jnp.zeros_like(low)], 0).astype(jnp.bfloat16)
    right = jnp.concatenate([weight, weight_low, weight, jnp.zeros_like(weight)], 0)
    total = lax.dot_general(
        left, right.astype(jnp.bfloat16), (((0,), (0,)), ((), ())), preferred_element_type=F32
    )
    energies = total.shape[1] // 2
    for part in range(2):
        out_ref[part] = total[: q * q, part * energies : (part + 1) * energies]


def jackson_weights(count):
    total = count + 1.0
    values = []
    for order in range(count):
        damping = (
            (count - order + 1.0) * math.cos(math.pi * order / total)
            + math.sin(math.pi * order / total) / math.tan(math.pi / total)
        ) / total
        values.append(damping if order == 0 else 2.0 * damping)
    return jnp.asarray(values, dtype=F32)


def energy_tables(energy_index, count, total_energies):
    phase = math.pi * (energy_index.astype(F32) + 0.5) / total_energies
    theta = jnp.arccos(energy_edge * jnp.cos(phase))
    orders = jnp.arange(count).astype(F32)
    weights = jackson_weights(count)
    angles = orders[:, None] * theta[None, :]
    denominator = jnp.sin(theta)[None, :]
    real_part = -weights[:, None] * jnp.sin(angles) / denominator
    imag_part = -weights[:, None] * jnp.cos(angles) / denominator
    return jnp.concatenate([real_part, imag_part], 1)


def add_over(value, axis):
    peers = lax.axis_size(axis)
    if peers & (peers - 1):
        return lax.psum(value, axis)
    if peers == 4:
        others = [lax.ppermute(value, axis, [(i, i ^ s) for i in range(peers)]) for s in (1, 2, 3)]
        return (value + others[0]) + (others[1] + others[2])
    shift = 1
    while shift < peers:
        value = value + lax.ppermute(value, axis, [(i, i ^ shift) for i in range(peers)])
        shift *= 2
    return value


VMEM = pl.BlockSpec(memory_space=pltpu.VMEM)
SMEM = pl.BlockSpec(memory_space=pltpu.SMEM)
HBM = pl.BlockSpec(memory_space=pltpu.MemorySpace.HBM)


def params(mib):
    return pltpu.CompilerParams(vmem_limit_bytes=mib * 2**20)


def send(array, axis, step):
    peers = lax.axis_size(axis)
    return lax.ppermute(array, axis, [(i, (i + step) % peers) for i in range(peers)])


def on_device(levels, probe_bits):
    count_gx = lax.axis_size("gx")
    count_gy = lax.axis_size("gy")
    d = Dims(levels, probe_bits, count_gx)
    sites = d.pl * d.total_rows * d.cols * count_gy
    first_row = (lax.axis_index("gx") * d.rows).astype(jnp.int32).reshape(1)
    in_hbm = lambda x: pltpu.with_memory_space_constraint(x, pltpu.MemorySpace.HBM)
    per_device = NE // (count_gx * count_gy)
    first_energy = (lax.axis_index("gx") * count_gy + lax.axis_index("gy")) * per_device
    first_energy = first_energy.astype(jnp.int32).reshape(1)
    bits = tile_view(probe_bits, (d.q, d.pl))
    levels = in_hbm(tile_view(levels, (d.pl,)))
    dma = pltpu.SemaphoreType.DMA
    padded = d.rows + 2 * STEPS
    vectors = [pltpu.VMEM((padded - 2 * n, d.pl, d.q, d.width), F32) for n in range(STEPS)]
    last = pltpu.VMEM((d.rows, d.pl, d.q, d.cols), F32)
    onsite = pltpu.VMEM((padded, d.pl, d.width), F32)
    gram_type = pltpu.VMEM(gram_shape(d), F32)
    tiles = lambda n: pltpu.VMEM((n, SUB, LANES), F32)

    ua = pl.pallas_call(
        functools.partial(first_kernel, d),
        out_shape=tiles(d.tiles("ua")), in_specs=[SMEM, SMEM, HBM], out_specs=VMEM,
        scratch_shapes=[pltpu.VMEM((d.pl, d.q, d.ct * SUB, LANES), jnp.int32), dma((d.pl,))],
        compiler_params=params(4), name="first",
    )(first_row, first_energy, in_hbm(bits))
    ua = send(ua, "gx", 1)
    v0, ons, da, right, left = pl.pallas_call(
        functools.partial(fill_kernel, d),
        out_shape=[vectors[0], onsite, tiles(d.tiles("da"))] + [tiles(d.edge_tiles)] * 2,
        in_specs=[SMEM, HBM, HBM], out_specs=[VMEM] * 5,
        scratch_shapes=[
            pltpu.VMEM((d.pl, d.q) + bits.shape[2:], jnp.int32), pltpu.VMEM(levels.shape, jnp.int32),
            dma((d.pl + 1,)),
        ],
        compiler_params=params(6), name="fill",
    )(first_row, in_hbm(bits), levels)
    before = send(right, "gy", 1)
    after = send(left, "gy", -1)
    v0, ons, da, ub, db, dc = pl.pallas_call(
        functools.partial(side_kernel, d),
        out_shape=[vectors[0], onsite] + [tiles(d.tiles(name)) for name in ("da", "ub", "db", "dc")],
        in_specs=[VMEM] * 5, out_specs=[VMEM] * 6,
        scratch_shapes=[pltpu.VMEM((3, d.pl, d.q, d.width), F32)],
        input_output_aliases={2: 0, 3: 1, 4: 2},
        compiler_params=params(3), name="side",
    )(before, after, v0, ons, da)
    ub = send(ub, "gx", 1)
    da = send(da, "gx", -1)
    db = send(db, "gx", -1)
    dc = send(dc, "gx", -1)
    *rest, gram = pl.pallas_call(
        functools.partial(interior_kernel, d),
        out_shape=vectors[1:] + [last, gram_type], in_specs=[VMEM] * 2, out_specs=[VMEM] * (STEPS + 1),
        compiler_params=params(3), name="interior",
    )(v0, ons)
    kept = [v0] + rest + [ons, gram]
    kinds = vectors + [last, onsite, gram_type]

    def wave(received, names, waves, kept, extra=(), specs=(), scratch=()):
        return pl.pallas_call(
            functools.partial(wave_kernel, d, names, waves),
            out_shape=kinds + list(extra), in_specs=[VMEM] * (len(names) + len(kept)),
            out_specs=[VMEM] * len(kept) + list(specs), scratch_shapes=list(scratch),
            input_output_aliases={len(names) + i: i for i in range(len(kept))},
            compiler_params=params(4),
        )(*received, *kept)

    every = tuple(("u", k) for k in range(1, STEPS + 1))
    stage_rows = (d.rt - 1) * d.ct * SUB
    *kept, lower = wave(
        [ua, ub], ("ua", "ub"), every, kept, [pltpu.HBM(bits.shape, F32)], [HBM],
        [pltpu.VMEM((d.pl, d.q, stage_rows, LANES), F32), dma((d.pl,))],
    )
    kept = wave([da], ("da",), (("d", 1), ("d", 2)), kept)
    *kept, _, gram = wave([db], ("db",), (("d", 3),), kept, [pltpu.VMEM((d.q, LANES), F32)], [VMEM])
    last_vector = pl.pallas_call(
        functools.partial(last_kernel, d),
        out_shape=[jax.ShapeDtypeStruct(bits.shape, F32)] + kinds[:-1],
        in_specs=[VMEM] * (len(kept) + 1) + [HBM], out_specs=[HBM] + [VMEM] * len(kept),
        scratch_shapes=[pltpu.VMEM((d.pl, d.q, d.ct * SUB, LANES), F32), dma((d.pl,))],
        input_output_aliases={**{1 + i: 1 + i for i in range(len(kept))}, len(kept) + 1: 0},
        compiler_params=params(4), name="last",
    )(dc, *kept, lower)[0]
    last_vector = untile_view(last_vector, probe_bits.shape)

    gram = add_over(add_over(gram, "gy"), "gx")
    tables = energy_tables(first_energy + jnp.arange(per_device), NMOM, NE)
    picks = pl.pallas_call(
        functools.partial(pick_kernel, d),
        out_shape=[pltpu.VMEM((LANES, 2 * NMOM * LANES), jnp.bfloat16)], out_specs=[VMEM],
        compiler_params=params(1), name="picks",
    )()[0]
    green = pl.pallas_call(
        functools.partial(green_kernel, d, sites),
        out_shape=jax.ShapeDtypeStruct((2, d.q * d.q, per_device), F32),
        in_specs=[VMEM] * 3, out_specs=VMEM, compiler_params=params(2), name="green",
    )(tables, picks, gram)
    return green.transpose(0, 2, 1), last_vector


def solution(mesh):
    placed = (P(None, "gx", "gy"), P(None, None, "gx", "gy"))
    return jax.shard_map(
        on_device,
        mesh=mesh,
        in_specs=placed,
        out_specs=(P(None, ("gx", "gy"), None), P(None, None, "gx", "gy")),
        check_vma=False,
    )
```

```python
import functools
import math

import jax
import jax.numpy as jnp
from jax import lax
from jax.experimental import pallas as pl
from jax.experimental.pallas import tpu as pltpu
from jax.sharding import PartitionSpec as P


STEPS = 4
LEVELS = 8
NE = 8192
NMOM = 2 * STEPS
LANES = 128
SUB = 8

disorder_width = 4.0
field_strength = 3.0
spectral_scale = 10.0
energy_edge = 0.9

F32 = jnp.float32


HOP = 2.0 / spectral_scale


def tile_view(array, lead):
    _, cols = array.shape[-2:]
    split = array.reshape(lead + (-1, SUB, cols // LANES, LANES))
    n = len(lead)
    return split.transpose(*range(n + 1), n + 2, n + 1, n + 3).reshape(lead + (-1, LANES))


def untile_view(view, shape):
    rows, cols = shape[-2:]
    split = view.reshape(-1, rows // SUB, cols // LANES, SUB, LANES)
    return split.transpose(0, 1, 3, 2, 4).reshape(shape)


class Rows:
    def __init__(self, ref, offset):
        self.ref, self.offset = ref, offset

    def __getitem__(self, index):
        if isinstance(index, tuple):
            return self.ref[(index[0] + self.offset,) + index[1:]]
        return self.ref[index + self.offset]

    def __setitem__(self, index, value):
        self.ref[(index[0] + self.offset,) + index[1:]] = value

    def rows(self, start, count):
        return self.ref.at[pl.ds(start + self.offset, count)]


def all_rows(refs):
    return tuple(Rows(ref, -n if n < STEPS else 0) for n, ref in enumerate(refs))


class Dims:
    def __init__(self, levels, bits, gx):
        self.q = bits.shape[0]
        self.pl, self.rows, self.cols = levels.shape
        self.ct = self.cols // LANES
        self.rt = self.rows // SUB
        self.width = self.cols + LANES
        self.total_rows = self.rows * gx
        self.row_tiles = self.pl * self.ct
        self.per_corner = LANES // (2 * STEPS)
        self.per_edge = LANES // STEPS
        self.edge_v = -(-self.rows * self.pl // self.per_edge)
        self.edge_tiles = self.edge_v + -(-self.rows // self.per_edge)
        self.plan = {
            "ua": (((0, 1), (0, 2)), 0, ()),
            "ub": (((1, 2), (2, 2)), 1, ((0, 1), (0, 2), (1, 2))),
            "da": (((0, 1), (0, 2)), 1, ((0, 1), (0, 2))),
            "db": (((1, 2),), 0, ((1, 2),)),
            "dc": (((2, 2),), 0, ()),
        }

    def places(self, name):
        rows, onsite, corners = self.plan[name]
        first = len(rows) * self.row_tiles
        second = first + onsite * self.ct
        third = second - (-len(corners) * self.pl // self.per_corner)
        return first, second, third, third + (onsite if corners else 0)

    def tiles(self, name):
        return self.places(name)[-1]

    def halo(self, name, k):
        return STEPS - k if name[0] == "u" else STEPS + self.rows - 1 + k

    def source(self, name, k):
        return STEPS + self.rows - k if name[0] == "u" else STEPS - 1 + k


def lanes_of(t):
    return slice(t * LANES, (t + 1) * LANES)


def to_spin(bits):
    return (2 * bits - 1).astype(F32)


def first_kernel(d, __, ___, bits_ref, out_ref, scratch, sem):
    size = d.ct * SUB
    copies = [
        pltpu.make_async_copy(
            bits_ref.at[:, p, pl.ds((d.rt - 1) * size, size)], scratch.at[p], sem.at[p]
        )
        for p in range(d.pl)
    ]
    for copy in copies:
        copy.start()
    for p, copy in enumerate(copies):
        copy.wait()
        flat = scratch.at[p].reshape(d.q * size, LANES)
        for i, (_, k) in enumerate(d.plan["ua"][0]):
            for t in range(d.ct):
                bits = flat[pl.ds(t * SUB + SUB - k, d.q, stride=size), :]
                out_ref[i * d.row_tiles + p * d.ct + t] = to_spin(bits)


def fill_kernel(
    d, row_ref, bits_ref, levels_ref, v_ref, ons_ref, da_ref, right_ref, left_ref, scratch, lscratch, sem
):
    lcopy = pltpu.make_async_copy(levels_ref, lscratch, sem.at[d.pl])
    copies = [
        pltpu.make_async_copy(bits_ref.at[:, p], scratch.at[p], sem.at[p]) for p in range(d.pl)
    ]
    lcopy.start()
    for copy in copies:
        copy.start()
    lcopy.wait()
    first_row = row_ref[0]
    for r in range(d.rt):
        for t in range(d.ct):
            level = lscratch[:, pl.ds((r * d.ct + t) * SUB, SUB), :].astype(F32)
            sub = lax.broadcasted_iota(jnp.int32, level.shape, 1)
            index = (first_row + r * SUB + sub).astype(F32)
            field = field_strength * ((index + 0.5) / d.total_rows - 0.5)
            onsite = disorder_width * (level / (LEVELS - 1) - 0.5) + field
            onsite = jnp.swapaxes(onsite * HOP, 0, 1)
            for i in range(SUB):
                ons_ref[STEPS + r * SUB + i, :, lanes_of(t)] = onsite[i]
    for p, copy in enumerate(copies):
        copy.wait()

        def block(r, _, p=p):
            for t in range(d.ct):
                start = pl.multiple_of((r * d.ct + t) * SUB, SUB)
                spins = jnp.swapaxes(to_spin(scratch[p, :, pl.ds(start, SUB), :]), 0, 1)
                v_ref[pl.ds(STEPS + r * SUB, SUB), p, :, lanes_of(t)] = spins
            return 0

        lax.fori_loop(0, d.rt, block, 0)
    lane = lax.broadcasted_iota(jnp.int32, (SUB, LANES), 1)
    low, high = lane < STEPS, lane >= LANES - STEPS

    def pack(items, ref, base, low_side):
        for at in range(0, len(items), d.per_edge):
            total = None
            for g, item in enumerate(items[at : at + d.per_edge]):
                tile = jnp.where(low if low_side else high, item(), 0.0)
                moved = pltpu.roll(tile, (STEPS * g + (0 if low_side else STEPS)) % LANES, 1)
                total = moved if total is None else total + moved
            ref[base + at // d.per_edge] = total

    for ref, t, low_side in ((right_ref, d.ct - 1, False), (left_ref, 0, True)):
        at = lanes_of(t)
        spins = [
            lambda r=r, p=p: v_ref[STEPS + r, p, :, at] for r in range(d.rows) for p in range(d.pl)
        ]
        pack(spins, ref, 0, low_side)
        onsite = [lambda r=r: ons_ref[STEPS + r, :, at] for r in range(d.rows)]
        pack(onsite, ref, d.edge_v, low_side)
    put_rows(d, "da", da_ref, {0: Rows(v_ref, 0)}, ons_ref)


def put_rows(d, name, ref, v, ons_ref):
    rows, onsite, _ = d.plan[name]
    for i, (n, k) in enumerate(rows):
        if n in v:
            for p in range(d.pl):
                for t in range(d.ct):
                    ref[i * d.row_tiles + p * d.ct + t] = v[n][d.source(name, k), p, :, lanes_of(t)]
    if onsite:
        for t in range(d.ct):
            ref[d.places(name)[0] + t] = ons_ref[d.source(name, 1), :, lanes_of(t)]


def side_kernel(
    d, before_ref, after_ref, v_in, o_in, da_in, v_ref, ons_ref, da_ref, ub_ref, db_ref, dc_ref, work
):
    lane = lax.broadcasted_iota(jnp.int32, (SUB, LANES), 1)
    low, high = lane < STEPS, lane >= LANES - STEPS

    def side(base, i):
        tile, g = base + i // d.per_edge, i % d.per_edge
        after = pltpu.roll(after_ref[tile], (-STEPS * g) % LANES, 1)
        before = pltpu.roll(before_ref[tile], (LANES - STEPS - STEPS * g) % LANES, 1)
        return jnp.where(low, after, jnp.where(high, before, 0.0))

    at = slice(d.cols, d.width)
    for r in range(d.rows):
        for p in range(d.pl):
            v_ref[STEPS + r, p, :, at] = side(0, r * d.pl + p)
        ons_ref[STEPS + r, :, at] = side(d.edge_v, r)
    v0 = Rows(v_ref, 0)
    for letter, named in (("u", {"ub": ub_ref}), ("d", {"da": da_ref, "db": db_ref, "dc": dc_ref})):
        second, third = d.source(letter, 2), d.source(letter, 3)
        v = (v0, Rows(work, -min(second, third)))
        for row in (third, second):
            one_row(d, 1, row, v, ons_ref)
        part = Rows(work, 2 - second)
        for p, value in enumerate(row_values(d, 2, second, v, ons_ref, leave=2 * second - third)):
            part[second, p] = value
        v = {0: v0, 1: v[1], 2: part}
        for name, ref in named.items():
            if name != "da":
                put_rows(d, name, ref, v, ons_ref)
            _, onsite, corners = d.plan[name]
            _, start, onsite_at, _ = d.places(name)
            packs = [(start, [(v[n], d.source(name, k), p) for n, k in corners for p in range(d.pl)])]
            for start, items in packs:
                for base in range(0, len(items), d.per_corner):
                    total = None
                    for g, (rows, row, p) in enumerate(items[base : base + d.per_corner]):
                        tile = jnp.where(low | high, rows[row, p, :, at], 0.0)
                        moved = pltpu.roll(tile, (STEPS + 2 * STEPS * g) % LANES, 1)
                        total = moved if total is None else total + moved
                    ref[start + base // d.per_corner] = total
            if onsite:
                ref[onsite_at] = ons_ref[d.source(name, 1), :, at]


def install(d, name, ref, v, ons_ref):
    rows, onsite, corners = d.plan[name]
    first, second, third, _ = d.places(name)
    for i, (n, k) in enumerate(rows):
        for p in range(d.pl):
            for t in range(d.ct):
                v[n][d.halo(name, k), p, :, lanes_of(t)] = ref[i * d.row_tiles + p * d.ct + t]
            if n == 2:
                v[n][d.halo(name, k), p, :, d.cols :] = jnp.zeros((d.q, LANES), F32)
    at = slice(d.cols, d.width)
    if onsite:
        for t in range(d.ct):
            ons_ref[d.halo(name, 1), :, lanes_of(t)] = ref[first + t]
        ons_ref[d.halo(name, 1), :, at] = ref[third]
    lane = lax.broadcasted_iota(jnp.int32, (SUB, LANES), 1)
    edge = (lane < STEPS) | (lane >= LANES - STEPS)
    for i, (n, k) in enumerate(corners):
        for p in range(d.pl):
            j = i * d.pl + p
            tile, g = second + j // d.per_corner, j % d.per_corner
            moved = pltpu.roll(ref[tile], (-(STEPS + 2 * STEPS * g)) % LANES, 1)
            v[n][d.halo(name, k), p, :, at] = jnp.where(edge, moved, 0.0)


def complete(d, letter, v):
    for p in range(d.pl):
        far, near = d.halo(letter, 2), d.halo(letter, 1)
        v[2][far, p] = v[2][far, p] - HOP * v[1][near, p]


def row_values(d, n, at, v, ons, leave=None):
    source = v[n - 1]
    values = []
    for p in range(d.pl):
        x = source[at, p]
        near = [source[row, p] for row in (at + 1, at - 1) if row != leave]
        beside = near[0] if leave is not None else near[0] + near[1]
        beside = beside + pltpu.roll(x, 1, 1) + pltpu.roll(x, d.width - 1, 1)
        if p + 1 < d.pl:
            beside = beside + source[at, p + 1]
        if p > 0:
            beside = beside + source[at, p - 1]
        value = ons[at, pl.ds(p, SUB, stride=0), :] * x - HOP * beside
        values.append(0.5 * value if n == 1 else value - v[n - 2][at, p])
    return values


def one_row(d, n, at, v, ons):
    for p, value in enumerate(row_values(d, n, at, v, ons)):
        if n < STEPS:
            v[n][at, p] = value
        else:
            v[n][at - STEPS, p] = value[:, : d.cols]


def split_pair(x):
    high = x.astype(jnp.bfloat16).astype(F32)
    return high, x - high


def gram_row(d, at, v, last):
    total = None
    for p in range(d.pl):
        spin = v[0][at, p, :, : d.cols]
        halves = [split_pair(v[m][at, p, :, : d.cols]) for m in range(1, STEPS)]
        halves.append(split_pair(last(p)))
        right = [spin, spin]
        for pair in halves:
            right += list(pair)
        third = halves[STEPS - 2]
        left = [spin, third[0], third[1], third[1]]
        right = jnp.concatenate(right, 0).astype(jnp.bfloat16)
        left = jnp.concatenate(left, 0).astype(jnp.bfloat16)
        part = lax.dot_general(
            left, right, (((1,), (1,)), ((), ())), preferred_element_type=F32
        )
        total = part if total is None else total + part
    return total[: 3 * d.q]


def gram_shape(d):
    return (3 * d.q, LANES)


def add_gram(gram_ref, part):
    gram_ref[:, : part.shape[1]] += part


def packed_gram(d, gram):
    q = d.q
    zero, high, low = gram[:q], gram[q : 2 * q], gram[2 * q :]
    lane = lax.broadcasted_iota(jnp.int32, zero.shape, 1)
    with_zero = jnp.where(lane < q, zero, zero + pltpu.roll(zero, LANES - q, 1))
    with_third = high + pltpu.roll(high, LANES - q, 1) + low
    return jnp.where(lane % (2 * q) < q, with_zero, pltpu.roll(with_third, q, 1))


def interior_kernel(d, v_ref, ons, *refs):
    v, gram_ref = all_rows((v_ref,) + refs[:STEPS]), refs[STEPS]
    gram_ref[...] = jnp.zeros(gram_ref.shape, F32)
    for n in range(1, STEPS + 1):

        def step(row, _, n=n):
            at = row + STEPS
            one_row(d, n, at, v, ons)
            if n == STEPS:
                add_gram(gram_ref, gram_row(d, at, v, lambda p: v[n][row, p]))
            return 0

        lax.fori_loop(n, d.rows - n, step, 0)


def wave_kernel(d, names, waves, *refs):
    recv = refs[: len(names)]
    refs = refs[len(names) + STEPS + 3 :]
    v = all_rows(refs[: STEPS + 1])
    ons, gram_ref, *extra = refs[STEPS + 1 :]
    for name, ref in zip(names, recv):
        install(d, name, ref, v, ons)

    def gram(at, last=None):
        part = gram_row(d, at, v, last or (lambda p: v[STEPS][at - STEPS, p]))
        add_gram(gram_ref, part)

    top = STEPS + d.rows - 1
    for side, k in waves:
        at_of = lambda n: STEPS + n - k if side == "u" else top - (n - k)
        if k == STEPS:
            complete(d, side, v)
        if side == "d" and k == STEPS - 1:
            for n in range(2, STEPS):
                for p in range(d.pl):
                    v[n][at_of(n), p] = v[n][at_of(n), p] - HOP * v[n - 1][at_of(n - 1), p]
        else:
            for n in range(max(1, k - 1), STEPS):
                one_row(d, n, at_of(n), v, ons)
        at = at_of(STEPS)
        if side == "u" or k < STEPS - 1:
            one_row(d, STEPS, at, v, ons)
            inner = HOP if side == "u" and k == STEPS else None
            gram(at, inner and (lambda p: v[STEPS][0, p] - inner * v[STEPS - 1][at - 1, p, :, : d.cols]))
    if ("u", STEPS) in waves:
        flush(d, v[STEPS], *extra)
    if ("d", STEPS - 2) in waves:
        for n in range(2, STEPS):
            at = top + STEPS - 1 - n
            for p, value in enumerate(row_values(d, n, at, v, ons, leave=at + 1)):
                v[n][at, p] = value
        for p, value in enumerate(row_values(d, STEPS, top - 1, v, ons, leave=top)):
            v[STEPS][d.rows - 2, p] = value[:, : d.cols]
        gram(top - 1)
    if ("d", STEPS - 1) in waves:
        for p, value in enumerate(row_values(d, STEPS, top, v, ons, leave=top + 1)):
            v[STEPS][d.rows - 1, p] = value[:, : d.cols]
        gram(top, lambda p: v[STEPS][d.rows - 1, p] - HOP * v[STEPS - 1][top - 1, p, :, : d.cols])
        extra[0][...] = packed_gram(d, gram_ref[...])


def transpose_tiles(d, r, p, rows, stage):
    for t in range(d.ct):
        tile = rows[:, :, lanes_of(t)]
        stage[p, :, pl.ds((r * d.ct + t) * SUB, SUB), :] = jnp.swapaxes(tile, 0, 1)


def flush(d, v4, out_ref, stage, sem):
    size = (d.rt - 1) * d.ct * SUB
    copies = []
    for p in range(d.pl):
        for r in range(d.rt - 1):
            transpose_tiles(d, r, p, v4.rows(r * SUB, SUB)[:, p], stage)
        copies.append(
            pltpu.make_async_copy(stage.at[p], out_ref.at[:, p, pl.ds(0, size)], sem.at[p])
        )
        copies[-1].start()
    for copy in copies:
        copy.wait()


def last_kernel(d, dc_ref, *refs):
    out_ref, *refs = refs[STEPS + 3 :]
    v, (ons, stage, sem) = all_rows(refs[: STEPS + 1]), refs[STEPS + 1 :]
    install(d, "dc", dc_ref, v, ons)
    complete(d, "d", v)
    top = STEPS + d.rows - 1
    one_row(d, STEPS - 1, top + 1, v, ons)
    copies = []
    size = d.ct * SUB
    for p in range(d.pl):
        for row in (d.rows - 2, d.rows - 1):
            above = v[STEPS - 1][row + STEPS + 1, p, :, : d.cols]
            v[STEPS][row, p] = v[STEPS][row, p] - HOP * above
        transpose_tiles(d, 0, p, v[STEPS].rows((d.rt - 1) * SUB, SUB)[:, p], stage)
        copies.append(pltpu.make_async_copy(
            stage.at[p], out_ref.at[:, p, pl.ds((d.rt - 1) * size, size)], sem.at[p]
        ))
        copies[-1].start()
    for copy in copies:
        copy.wait()


def moment_blocks():
    return [2 * m for m in range(STEPS)] + [2 * m + 1 for m in range(1, STEPS + 1)]


def pick_kernel(d, out_ref):
    column = lax.broadcasted_iota(jnp.int32, (LANES, LANES), 0)
    lane = lax.broadcasted_iota(jnp.int32, (LANES, LANES), 1)
    for i, block in enumerate(moment_blocks()):
        for turned, index in enumerate((lane % d.q, lane // d.q)):
            hit = (column == block * d.q + index) & (lane < d.q * d.q)
            out_ref[:, lanes_of(2 * i + turned)] = jnp.where(hit, 1.0, 0.0).astype(jnp.bfloat16)


def green_kernel(d, sites, tables_ref, picks_ref, packed_ref, out_ref):
    q = d.q
    rest = packed_ref[...]
    parts = []
    for _ in range(3):
        parts.append(rest.astype(jnp.bfloat16).astype(F32))
        rest = rest - parts[-1]
    left = jnp.concatenate(parts + [jnp.zeros_like(rest)], 0).astype(jnp.bfloat16)
    sub = lax.broadcasted_iota(jnp.int32, (q, LANES), 0)
    out_lane = lax.broadcasted_iota(jnp.int32, (q, LANES), 1)
    wide = jnp.dot(left, picks_ref[...], preferred_element_type=F32)
    wide = wide[:q] + wide[q : 2 * q] + wide[2 * q : 3 * q]
    straight, turned = sub == out_lane // q, sub == out_lane % q
    flat = []
    for i in range(len(moment_blocks())):
        one = jnp.where(straight, wide[:, lanes_of(2 * i)], 0.0)
        two = jnp.where(turned, wide[:, lanes_of(2 * i + 1)], 0.0)
        flat.append(jnp.sum(one + two, 0, keepdims=True) * (0.5 / sites))
    moments = flat[:STEPS]
    for m, base in ((0, 2), (1, 1), (2, 0), (3, 1)):
        moments.append(2.0 * flat[STEPS + m] - moments[base])
    high, low = split_pair(jnp.concatenate(moments, 0))
    weight, weight_low = split_pair(tables_ref[...])
    left = jnp.concatenate([high, high, low, jnp.zeros_like(low)], 0).astype(jnp.bfloat16)
    right = jnp.concatenate([weight, weight_low, weight, jnp.zeros_like(weight)], 0)
    total = lax.dot_general(
        left, right.astype(jnp.bfloat16), (((0,), (0,)), ((), ())), preferred_element_type=F32
    )
    energies = total.shape[1] // 2
    for part in range(2):
        out_ref[part] = total[: q * q, part * energies : (part + 1) * energies]


def jackson_weights(count):
    total = count + 1.0
    values = []
    for order in range(count):
        damping = (
            (count - order + 1.0) * math.cos(math.pi * order / total)
            + math.sin(math.pi * order / total) / math.tan(math.pi / total)
        ) / total
        values.append(damping if order == 0 else 2.0 * damping)
    return jnp.asarray(values, dtype=F32)


def energy_tables(energy_index, count, total_energies):
    phase = math.pi * (energy_index.astype(F32) + 0.5) / total_energies
    theta = jnp.arccos(energy_edge * jnp.cos(phase))
    orders = jnp.arange(count).astype(F32)
    weights = jackson_weights(count)
    angles = orders[:, None] * theta[None, :]
    denominator = jnp.sin(theta)[None, :]
    real_part = -weights[:, None] * jnp.sin(angles) / denominator
    imag_part = -weights[:, None] * jnp.cos(angles) / denominator
    return jnp.concatenate([real_part, imag_part], 1)


def add_over(value, axis):
    peers = lax.axis_size(axis)
    if peers & (peers - 1):
        return lax.psum(value, axis)
    if peers == 4:
        others = [lax.ppermute(value, axis, [(i, i ^ s) for i in range(peers)]) for s in (1, 2, 3)]
        return (value + others[0]) + (others[1] + others[2])
    shift = 1
    while shift < peers:
        value = value + lax.ppermute(value, axis, [(i, i ^ shift) for i in range(peers)])
        shift *= 2
    return value


VMEM = pl.BlockSpec(memory_space=pltpu.VMEM)
SMEM = pl.BlockSpec(memory_space=pltpu.SMEM)
HBM = pl.BlockSpec(memory_space=pltpu.MemorySpace.HBM)


def params(mib):
    return pltpu.CompilerParams(vmem_limit_bytes=mib * 2**20)


def send(array, axis, step):
    peers = lax.axis_size(axis)
    return lax.ppermute(array, axis, [(i, (i + step) % peers) for i in range(peers)])


def on_device(levels, probe_bits):
    count_gx = lax.axis_size("gx")
    count_gy = lax.axis_size("gy")
    d = Dims(levels, probe_bits, count_gx)
    sites = d.pl * d.total_rows * d.cols * count_gy
    first_row = (lax.axis_index("gx") * d.rows).astype(jnp.int32).reshape(1)
    in_hbm = lambda x: pltpu.with_memory_space_constraint(x, pltpu.MemorySpace.HBM)
    per_device = NE // (count_gx * count_gy)
    first_energy = (lax.axis_index("gx") * count_gy + lax.axis_index("gy")) * per_device
    first_energy = first_energy.astype(jnp.int32).reshape(1)
    bits = tile_view(probe_bits, (d.q, d.pl))
    levels = in_hbm(tile_view(levels, (d.pl,)))
    dma = pltpu.SemaphoreType.DMA
    padded = d.rows + 2 * STEPS
    vectors = [pltpu.VMEM((padded - 2 * n, d.pl, d.q, d.width), F32) for n in range(STEPS)]
    last = pltpu.VMEM((d.rows, d.pl, d.q, d.cols), F32)
    onsite = pltpu.VMEM((padded, d.pl, d.width), F32)
    gram_type = pltpu.VMEM(gram_shape(d), F32)
    tiles = lambda n: pltpu.VMEM((n, SUB, LANES), F32)

    ua = pl.pallas_call(
        functools.partial(first_kernel, d),
        out_shape=tiles(d.tiles("ua")), in_specs=[SMEM, SMEM, HBM], out_specs=VMEM,
        scratch_shapes=[pltpu.VMEM((d.pl, d.q, d.ct * SUB, LANES), jnp.int32), dma((d.pl,))],
        compiler_params=params(4), name="first",
    )(first_row, first_energy, in_hbm(bits))
    ua = send(ua, "gx", 1)
    v0, ons, da, right, left = pl.pallas_call(
        functools.partial(fill_kernel, d),
        out_shape=[vectors[0], onsite, tiles(d.tiles("da"))] + [tiles(d.edge_tiles)] * 2,
        in_specs=[SMEM, HBM, HBM], out_specs=[VMEM] * 5,
        scratch_shapes=[
            pltpu.VMEM((d.pl, d.q) + bits.shape[2:], jnp.int32), pltpu.VMEM(levels.shape, jnp.int32),
            dma((d.pl + 1,)),
        ],
        compiler_params=params(6), name="fill",
    )(first_row, in_hbm(bits), levels)
    before = send(right, "gy", 1)
    after = send(left, "gy", -1)
    v0, ons, da, ub, db, dc = pl.pallas_call(
        functools.partial(side_kernel, d),
        out_shape=[vectors[0], onsite] + [tiles(d.tiles(name)) for name in ("da", "ub", "db", "dc")],
        in_specs=[VMEM] * 5, out_specs=[VMEM] * 6,
        scratch_shapes=[pltpu.VMEM((3, d.pl, d.q, d.width), F32)],
        input_output_aliases={2: 0, 3: 1, 4: 2},
        compiler_params=params(3), name="side",
    )(before, after, v0, ons, da)
    ub = send(ub, "gx", 1)
    da = send(da, "gx", -1)
    db = send(db, "gx", -1)
    dc = send(dc, "gx", -1)
    *rest, gram = pl.pallas_call(
        functools.partial(interior_kernel, d),
        out_shape=vectors[1:] + [last, gram_type], in_specs=[VMEM] * 2, out_specs=[VMEM] * (STEPS + 1),
        compiler_params=params(3), name="interior",
    )(v0, ons)
    kept = [v0] + rest + [ons, gram]
    kinds = vectors + [last, onsite, gram_type]

    def wave(received, names, waves, kept, extra=(), specs=(), scratch=()):
        return pl.pallas_call(
            functools.partial(wave_kernel, d, names, waves),
            out_shape=kinds + list(extra), in_specs=[VMEM] * (len(names) + len(kept)),
            out_specs=[VMEM] * len(kept) + list(specs), scratch_shapes=list(scratch),
            input_output_aliases={len(names) + i: i for i in range(len(kept))},
            compiler_params=params(4),
        )(*received, *kept)

    every = tuple(("u", k) for k in range(1, STEPS + 1))
    stage_rows = (d.rt - 1) * d.ct * SUB
    *kept, lower = wave(
        [ua, ub], ("ua", "ub"), every, kept, [pltpu.HBM(bits.shape, F32)], [HBM],
        [pltpu.VMEM((d.pl, d.q, stage_rows, LANES), F32), dma((d.pl,))],
    )
    kept = wave([da], ("da",), (("d", 1), ("d", 2)), kept)
    *kept, _, gram = wave([db], ("db",), (("d", 3),), kept, [pltpu.VMEM((d.q, LANES), F32)], [VMEM])
    last_vector = pl.pallas_call(
        functools.partial(last_kernel, d),
        out_shape=[jax.ShapeDtypeStruct(bits.shape, F32)] + kinds[:-1],
        in_specs=[VMEM] * (len(kept) + 1) + [HBM], out_specs=[HBM] + [VMEM] * len(kept),
        scratch_shapes=[pltpu.VMEM((d.pl, d.q, d.ct * SUB, LANES), F32), dma((d.pl,))],
        input_output_aliases={**{1 + i: 1 + i for i in range(len(kept))}, len(kept) + 1: 0},
        compiler_params=params(4), name="last",
    )(dc, *kept, lower)[0]
    last_vector = untile_view(last_vector, probe_bits.shape)

    gram = add_over(add_over(gram, "gy"), "gx")
    tables = energy_tables(first_energy + jnp.arange(per_device), NMOM, NE)
    picks = pl.pallas_call(
        functools.partial(pick_kernel, d),
        out_shape=[pltpu.VMEM((LANES, 2 * NMOM * LANES), jnp.bfloat16)], out_specs=[VMEM],
        compiler_params=params(1), name="picks",
    )()[0]
    green = pl.pallas_call(
        functools.partial(green_kernel, d, sites),
        out_shape=jax.ShapeDtypeStruct((2, d.q * d.q, per_device), F32),
        in_specs=[VMEM] * 3, out_specs=VMEM, compiler_params=params(2), name="green",
    )(tables, picks, gram)
    return green.transpose(0, 2, 1), last_vector


def solution(mesh):
    placed = (P(None, "gx", "gy"), P(None, None, "gx", "gy"))
    return jax.shard_map(
        on_device,
        mesh=mesh,
        in_specs=placed,
        out_specs=(P(None, ("gx", "gy"), None), P(None, None, "gx", "gy")),
        check_vma=False,
    )
```
